32 devices in a mesh: tile: 8 (over z, y), frame: 4 (over x, core).
Axes of the slice: x: 2, y: 2, z: 4, core: 2. Of those that a mesh axis runs over, the one named last changes fastest.
Arguments:
- recording: bfloat16 [8192, 512], P('tile', 'frame'), may hold values from 0 to 2
- footprints: bfloat16 [8192, 128], P('tile'), may hold values from 0 to 10, as said below
- slot_owner: int32 [1024, 1], P('tile'), may hold values from 0 to 7; in each aligned block of 128 rows (0 to 127, 128 to 255, ...) at most 32 rows name the same one
- slot_pick: int32 [1024], P('tile'), may hold values from 0 to 39
- traces: float32 [2560, 512], P('tile', 'frame'), may hold values from 0 to 1
Outputs:
- new_traces: float32 [2560, 512], P('tile', 'frame')
- new_footprints: bfloat16 [8192, 128], P('tile')
The draws below stay inside these ranges and needn't reach their ends.
Inputs may be any that keep to these rules, and one draw needn't show every extreme that they name: `footprints`: nonnegative; a slot's nonzero entries mark its footprint's support, all other entries are exactly zero. `slot_owner`: of the 128 slots of one tile no owner is named by more than 32, a bound that some block reaches.
All inputs are finite; a program needn't handle non-finite values.
Results may differ from the reference program's by a relative error of at most 0.003.
Values may be sent and summed in bfloat16 or wider, within the bound.
No kernel may reach another device: no remote copies, remote signals or barrier semaphores. Data moves between devices by JAX's collectives and lax.ppermute only.
A program may use at most 64 MiB of HBM per device.

```python
import math
import jax
import jax.numpy as jnp
import numpy as np
from jax import lax

K = 128
NO = 320
V_DEV = 1024
ITER_C = 4
ITER_A = 8
CAP = 32
VOXELS = 8192
FRAMES = 512
NEUR = 2560
SLOTS = 1024
N_TILE = 8


def draw_footprints(key, part):
    key_start, key_length, key_value, key_scale = jax.random.split(key, 4)
    start_cell = jax.random.randint(key_start, (N_TILE, 1, K), 0, V_DEV)
    run_length = jax.random.randint(key_length, (N_TILE, 1, K), V_DEV // 8, V_DEV // 2 + 1)
    voxel_index = jnp.arange(V_DEV, dtype=jnp.int32)[None, :, None]
    offset = (voxel_index - start_cell) % V_DEV
    support = offset < run_length
    values = jax.random.uniform(key_value, (N_TILE, V_DEV, K), jnp.float32, 0.2, 1.0)
    column_scale = jnp.exp(jax.random.uniform(key_scale, (N_TILE, 1, K), jnp.float32, 0.0, math.log(10.0)))
    values = values * column_scale
    return jnp.where(support, values, 0.0).reshape(VOXELS, K).astype(jnp.bfloat16)


def draw_traces(key, part):
    values = jax.random.uniform(jax.random.fold_in(key, 7), (NEUR, FRAMES), jnp.float32, 0.0, 1.0)
    local_index = jnp.arange(NEUR, dtype=jnp.int32) % NO
    active = local_index < max(2, NO // 8)
    level = jnp.where(active, 1.0, 0.1).astype(jnp.float32)
    return (values * level[:, None]).astype(jnp.float32)


def plant(array, stream_key, least, high):
    index_at = [jax.random.randint(jax.random.fold_in(stream_key, axis), (), 0, length) for axis, length in enumerate(array.shape)]
    widest = array.shape.index(max(array.shape))
    neighbour = index_at[:widest] + [(index_at[widest] + 1) % array.shape[widest]] + index_at[widest + 1:]
    return array.at[tuple(index_at)].set(least).at[tuple(neighbour)].set(high)


def shard_levels(rng, shape, cuts, low, top_value):
    def one(axis_at, shards_of):
        steps = jax.random.uniform(jax.random.fold_in(jax.random.fold_in(rng, 6), axis_at), (shards_of,), jnp.float32, low / len(cuts), top_value / len(cuts))
        return jnp.repeat(jnp.exp(steps), shape[axis_at] // shards_of).reshape((-1,) + (1,) * (len(shape) - axis_at - 1))

    loudness = one(*cuts[0])
    for cut in cuts[1:]:
        loudness = loudness * one(*cut)
    return loudness


def routed_block(key, own, number, rows, number_of, top, bound, lean):
    sequence = jax.random.permutation(key, number_of)
    crowded, usual = portions_of(number_of, rows * top, bound, lean, True), portions_of(number_of, rows * top, bound, lean, False)
    places = jnp.arange(number_of)

    def named(sizes, turn):
        used = int((sizes > 0).sum())
        fixed = max(1, used // 4)
        moved = fixed + (places - fixed + turn * (used - fixed)) % max(1, number_of - fixed)
        return jnp.zeros((number_of,), jnp.int32).at[sequence[jnp.where(places < fixed, places, moved)]].set(jnp.asarray(sizes, jnp.int32))

    sizes = jnp.where(number % 4 == 0, named(crowded, number // 4), named(usual, number - number // 4 - 1))
    mixed = jax.random.permutation(jax.random.fold_in(own, 3), number_of)
    source_of, sink = mixed[0:number_of // 2 * 2:2], mixed[1:number_of // 2 * 2:2]
    slack = jnp.minimum(sizes[source_of] - 1, bound - sizes[sink]) // 2
    slack = jnp.where((source_of == sequence[0]) | (sink == sequence[0]) | (sizes[sink] == 0), 0, jnp.maximum(slack, 0))
    moved = jax.random.randint(jax.random.fold_in(own, 4), (number_of // 2,), 0, 1 << 20) % (slack + 1)
    sizes = sizes.at[source_of].add(-moved).at[sink].add(moved)
    members = jnp.searchsorted(jnp.cumsum(sizes), jnp.arange(rows * top), side="right").astype(jnp.int32)
    listing = members.reshape(top, rows).T
    listing = listing[jax.random.permutation(jax.random.fold_in(own, 1), rows)]
    turn = jax.random.randint(jax.random.fold_in(own, 2), (rows, 1), 0, top)
    return jnp.take_along_axis(listing, (jnp.arange(top)[None, :] + turn) % top, axis=1)


def portions_of(count, total, most, lean, full):
    loads = [(1 << 20) // math.isqrt(standing ** lean) + 1 for standing in range(1, count + 1)]
    largest = most if full else min(most, max(-(-total // count), total * loads[0] // sum(loads)))
    least = 1 if total - largest >= count - 1 else 0
    given, rest = [largest] + [least] * (count - 1), total - largest - least * (count - 1)
    while rest > 0:
        movable = [i for i in range(1, count) if given[i] < largest] or [i for i in range(1, count) if given[i] < most]
        mass, left = sum([loads[i] for i in movable]), rest
        for i in movable:
            more = min(most - given[i], max(1, left * loads[i] // mass), rest)
            given[i] = given[i] + more
            rest = rest - more
    return np.array(given)


def setup_inputs(seed: int = 0) -> dict:
    keys = jax.random.split(jax.random.key(seed), 6)
    recording = jnp.clip(2.0 * jax.random.uniform(keys[0], (VOXELS, FRAMES), jnp.float32) ** shard_levels(keys[0], (VOXELS, FRAMES), ((0, 8), (1, 4)), -0.2, 0.2), 0.0, 2.0).astype(jnp.bfloat16)
    footprints = draw_footprints(jax.random.fold_in(keys[5], 71), 0)
    slot_owner_keys = jax.random.split(jax.random.fold_in(keys[2], 1), SLOTS // K)
    slot_owner_turns = jax.random.permutation(jax.random.fold_in(keys[2], 3), SLOTS // K)
    slot_owner = jax.vmap(lambda own, number: routed_block(jax.random.fold_in(keys[2], 2), own, number, K, N_TILE, 1, CAP, 2))(slot_owner_keys, slot_owner_turns).reshape((SLOTS, 1))
    slot_pick = plant(jax.random.randint(keys[3], (SLOTS,), 0, max(2, NO // 8)), jax.random.fold_in(keys[3], 1), 0, (max(2, NO // 8)) - 1).astype(jnp.int32)
    traces = draw_traces(jax.random.fold_in(keys[5], 71), 0)
    return dict(recording=recording, footprints=footprints, slot_owner=slot_owner, slot_pick=slot_pick, traces=traces)


def tile_stats(pair):
    block, data = pair
    gram = lax.dot_general(block, block, (((0,), (0,)), ((), ())), preferred_element_type=jnp.float32)
    drive = lax.dot_general(block, data, (((0,), (0,)), ((), ())), preferred_element_type=jnp.float32)
    return gram, drive


def footprint_steps(triple):
    block, data, slot_traces = triple
    slot_low = slot_traces.astype(jnp.bfloat16)
    data_sum = lax.dot_general(data, slot_low, (((1,), (1,)), ((), ())), preferred_element_type=jnp.float32)
    trace_gram = jnp.dot(slot_traces, slot_traces.T, precision=lax.Precision.HIGHEST)
    column_step = 1.0 / (1.0 + jnp.sum(jnp.abs(trace_gram), axis=1))
    support = block > 0
    iterate = block.astype(jnp.float32)
    for sweep in range(ITER_A):
        moved = iterate - (jnp.dot(iterate, trace_gram, precision=lax.Precision.HIGHEST) - data_sum) * column_step[None, :]
        iterate = jnp.where(support, jnp.maximum(moved, 0.0), jnp.zeros_like(moved))
    return iterate.astype(jnp.bfloat16)


def reference(recording, footprints, slot_owner, slot_pick, traces):
    neuron_row = (slot_owner[:, 0] * NO + slot_pick).astype(jnp.int32)
    blocks = footprints.reshape(N_TILE, V_DEV, K)
    datas = recording.reshape(N_TILE, V_DEV, FRAMES)
    gram, drive = lax.map(tile_stats, (blocks, datas))
    row_bound = jnp.sum(jnp.abs(gram), axis=2).reshape(-1)
    bound_sum = jax.ops.segment_sum(row_bound, neuron_row, num_segments=NEUR)
    scale_row = 1.0 / (1.0 + bound_sum)
    current = traces
    for iteration in range(ITER_C):
        slot_traces = current[neuron_row].reshape(N_TILE, K, FRAMES)
        terms = jnp.einsum("tkj,tjf->tkf", gram, slot_traces, precision=lax.Precision.HIGHEST) - drive
        grad_sum = jax.ops.segment_sum(terms.reshape(SLOTS, FRAMES), neuron_row, num_segments=NEUR)
        current = jnp.maximum(current - grad_sum * scale_row[:, None], 0.0)
    slot_traces = current[neuron_row].reshape(N_TILE, K, FRAMES)
    updated = lax.map(footprint_steps, (blocks, datas, slot_traces))
    return current, updated.reshape(VOXELS, K)
```

```python
import functools

import jax
import jax.numpy as jnp
from jax import lax
from jax.experimental import pallas as pl
from jax.experimental.pallas import tpu as pltpu
from jax.sharding import PartitionSpec as P

ITER_C = 4
ITER_A = 8
META = 8
DENSE_LIMIT = 1024
BF = jnp.bfloat16
F32 = jnp.float32
VMEM = pl.BlockSpec(memory_space=pltpu.VMEM)
SMEM = pl.BlockSpec(memory_space=pltpu.SMEM)
HIGHEST = lax.Precision.HIGHEST


def dot(a, b, ca, cb, precision=None):
    return lax.dot_general(a, b, (((ca,), (cb,)), ((), ())), precision=precision, preferred_element_type=F32)


def split(x):
    high = x.astype(BF)
    return high, (x - high.astype(F32)).astype(BF)


def pack_kernel(foot_ref, rec_ref, owner_ref, pick_ref, traces_ref, out_ref):
    tiles = out_ref.shape[0]
    slots = foot_ref.shape[1]
    active = traces_ref.shape[0] // 8
    foot = foot_ref[...]
    gram = dot(foot, foot, 0, 0)
    drive = dot(foot, rec_ref[...], 0, 0)
    bound = jnp.sum(jnp.abs(gram), axis=0, keepdims=True)
    high = bound.astype(BF).astype(F32)
    middle = (bound - high).astype(BF).astype(F32)
    low = bound - high - middle
    named = [high, middle, low, owner_ref[...].astype(F32), pick_ref[...].astype(F32)]
    rest = jnp.zeros((META - len(named), slots), F32)
    tail = jnp.concatenate([traces_ref[:active, :]] + named + [rest], axis=0).astype(BF)
    gram = gram.astype(BF)
    drive = drive.astype(BF)
    for tile in range(tiles):
        out_ref[tile, 0:slots, :] = gram
        out_ref[tile, slots : 2 * slots, :] = drive
        out_ref[tile, 2 * slots : 2 * slots + active + META, :] = tail


def gathered_parts(block, slots, active):
    gram = block[:slots]
    drive = block[slots : 2 * slots]
    tail = block[2 * slots :].astype(F32)
    meta = tail[active : active + META]
    return gram, drive, tail[:active], meta


def trace_kernel(tile_ref, got_ref, owner_ref, pick_ref, traces_ref, new_ref, own_ref, cur_ref):
    tiles = got_ref.shape[0]
    slots = got_ref.shape[2]
    active = traces_ref.shape[0] // 8
    count = tiles * active
    me = tile_ref[0]
    row = lax.broadcasted_iota(jnp.int32, (count, slots), 0).astype(F32)
    picks, bounds, mixed, drives = [], None, [], []
    for tile in range(tiles):
        gram, drive, first, meta = gathered_parts(got_ref[tile], slots, active)
        cur_ref[tile * active : (tile + 1) * active, :] = first
        hit = row == meta[3:4] * float(active) + meta[4:5]
        pick = jnp.where(hit, 1.0, 0.0)
        bound = pick * (meta[0:1] + meta[1:2] + meta[2:3])
        bounds = bound if bounds is None else bounds + bound
        pick = pick.astype(BF)
        picks.append(pick)
        drives.append(drive)
        mixed.append(dot(pick, gram, 1, 0))
    pick = jnp.concatenate(picks, axis=1)
    mixed = jnp.concatenate(mixed, axis=1)
    mixed_high, mixed_low = split(mixed)
    whole = dot(mixed_high, pick, 1, 1) + dot(mixed_low, pick, 1, 1)
    pull = dot(pick, jnp.concatenate(drives, axis=0), 1, 0)
    scale = 1.0 / (1.0 + jnp.sum(bounds, axis=1, keepdims=True))
    at = pl.multiple_of(me * active, 8)
    cur_ref[pl.ds(at, active), :] = traces_ref[:active, :]
    current = cur_ref[...]
    for _ in range(ITER_C):
        current = jnp.maximum(current - (dot(whole, current, 1, 0, HIGHEST) - pull) * scale, 0.0)
    cur_ref[...] = current
    new_ref[:active, :] = cur_ref[pl.ds(at, active), :]
    new_ref[active:, :] = jnp.maximum(traces_ref[active:, :], 0.0)
    own = jnp.where(row == (owner_ref[...] * active + pick_ref[...]).astype(F32), 1.0, 0.0)
    own_ref[...] = dot(own, current, 0, 0, HIGHEST)


def trace_steps_wide(got, owner, pick, traces, me):
    tiles, _, slots = got.shape
    active = traces.shape[0] // 8
    frames = traces.shape[1]
    gram, drive, first, meta = jax.vmap(lambda b: gathered_parts(b, slots, active))(got)
    index = (meta[:, 3] * active + meta[:, 4]).astype(jnp.int32).reshape(-1)
    bound = jax.ops.segment_sum((meta[:, 0] + meta[:, 1] + meta[:, 2]).reshape(-1), index, num_segments=tiles * active)
    scale = (1.0 / (1.0 + bound))[:, None]
    current = first.reshape(tiles * active, frames)
    current = lax.dynamic_update_slice(current, traces[:active], (me * active, 0))

    def step(_, current):
        taken = jnp.take(current, index, axis=0).reshape(tiles, slots, frames)
        terms = jnp.einsum("tkj,tjf->tkf", gram.astype(F32), taken, precision=HIGHEST) - drive.astype(F32)
        total = jax.ops.segment_sum(terms.reshape(-1, frames), index, num_segments=tiles * active)
        return jnp.maximum(current - total * scale, 0.0)

    current = lax.fori_loop(0, ITER_C, step, current)
    mine = lax.dynamic_slice(current, (me * active, 0), (active, frames))
    new = jnp.concatenate([mine, jnp.maximum(traces[active:], 0.0)], axis=0)
    own = jnp.take(current, owner[0] * active + pick[0], axis=0)
    return new, own


def partial_kernel(core_ref, rec_ref, own_ref, send_ref, keep_ref, gram_ref):
    half = keep_ref.shape[0]
    slots = own_ref.shape[0]
    core = core_ref[0]
    own = own_ref[...]
    low = own.astype(BF)
    here = pl.multiple_of(core * half, 16)
    there = pl.multiple_of((1 - core) * half, 16)
    gram = dot(own, own, 1, 1, HIGHEST)
    gram_ref[...] = gram
    gram_high, gram_low = split(gram)
    send_ref[half : half + slots, :] = gram_high
    send_ref[half + slots :, :] = gram_low
    send_ref[:half, :] = dot(rec_ref[pl.ds(there, half), :], low, 1, 1).astype(BF)
    keep_ref[...] = dot(rec_ref[pl.ds(here, half), :], low, 1, 1)


def join_kernel(keep_ref, gram_ref, got_ref, out_ref):
    half, slots = keep_ref.shape[0], gram_ref.shape[0]
    out_ref[:half, :] = (keep_ref[...] + got_ref[:half, :].astype(F32)).astype(BF)
    far = got_ref[half : half + slots, :].astype(F32) + got_ref[half + slots :, :].astype(F32)
    out_ref[half:, :] = (gram_ref[...] + far).astype(BF)


def sweep_kernel(core_ref, foot_ref, *refs):
    parts, out_ref = refs[:-1], refs[-1]
    half, slots = out_ref.shape
    total = parts[0][...].astype(F32)
    for part in parts[1:]:
        total = total + part[...].astype(F32)
    data, gram = total[:half], total[half:]
    here = pl.multiple_of(core_ref[0] * half, 16)
    foot = foot_ref[pl.ds(here, half), :].astype(F32)
    support = foot > 0
    step = 1.0 / (1.0 + jnp.sum(jnp.abs(gram), axis=0, keepdims=True))
    iterate = foot
    for _ in range(ITER_A):
        moved = iterate - (dot(iterate, gram, 1, 0, HIGHEST) - data) * step
        iterate = jnp.where(support, jnp.maximum(moved, 0.0), 0.0)
    out_ref[...] = iterate.astype(BF)


def body(recording, footprints, slot_owner, slot_pick, traces):
    tiles = lax.axis_size("tile")
    lanes = lax.axis_size("frame")
    voxels, slots = footprints.shape
    owned, frames = traces.shape
    active = owned // 8
    half = voxels // 2
    me = lax.axis_index("tile")
    spot = lax.axis_index("frame")
    core = (spot % 2).astype(jnp.int32)[None]
    owner = slot_owner.reshape(1, slots)
    pick = slot_pick.reshape(1, slots)
    rows = 2 * slots + active + META
    packed = pl.pallas_call(
        pack_kernel,
        out_shape=jax.ShapeDtypeStruct((tiles, rows, slots), BF),
        in_specs=[VMEM] * 5,
        out_specs=VMEM,
        name="pack",
    )(footprints, recording, owner, pick, traces)
    got = lax.all_to_all(packed, "tile", split_axis=0, concat_axis=0, tiled=True)
    if tiles * active <= DENSE_LIMIT:
        new_traces, own = pl.pallas_call(
            trace_kernel,
            out_shape=(jax.ShapeDtypeStruct((owned, frames), F32), jax.ShapeDtypeStruct((slots, frames), F32)),
            in_specs=[SMEM] + [VMEM] * 4,
            out_specs=(VMEM, VMEM),
            scratch_shapes=[pltpu.VMEM((tiles * active, frames), F32)],
            name="traces",
        )(me.astype(jnp.int32)[None], got, owner, pick, traces)
    else:
        new_traces, own = trace_steps_wide(got, owner, pick, traces, me)
    send, keep, gram = pl.pallas_call(
        partial_kernel,
        out_shape=(
            jax.ShapeDtypeStruct((half + 2 * slots, slots), BF),
            jax.ShapeDtypeStruct((half, slots), F32),
            jax.ShapeDtypeStruct((slots, slots), F32),
        ),
        in_specs=[SMEM, VMEM, VMEM],
        out_specs=(VMEM, VMEM, VMEM),
        name="partials",
    )(core, recording, own)

    def swap(value, bit):
        return lax.ppermute(value, "frame", [(i, i ^ bit) for i in range(lanes)])

    part = pl.pallas_call(
        join_kernel,
        out_shape=jax.ShapeDtypeStruct((half + slots, slots), BF),
        in_specs=[VMEM] * 3,
        out_specs=VMEM,
        name="join",
    )(keep, gram, swap(send, 1))
    parts = [part] + [swap(part, bit) for bit in range(2, lanes, 2)]
    mine = pl.pallas_call(
        sweep_kernel,
        out_shape=jax.ShapeDtypeStruct((half, slots), BF),
        in_specs=[SMEM] + [VMEM] * (1 + len(parts)),
        out_specs=VMEM,
        name="sweeps",
    )(core, footprints, *parts)
    other = swap(mine, 1)
    first = spot % 2 == 0
    updated = jnp.concatenate([jnp.where(first, mine, other), jnp.where(first, other, mine)], axis=0)
    return (new_traces, updated)


def solution(mesh):
    in_specs = (P("tile", "frame"), P("tile", None), P("tile", None), P("tile"), P("tile", "frame"))
    out_specs = (P("tile", "frame"), P("tile", None))
    return jax.shard_map(body, mesh=mesh, in_specs=in_specs, out_specs=out_specs, check_vma=False)
```

```python
import jax
import jax.numpy as jnp
from jax import lax
from jax.experimental import pallas as pl
from jax.experimental.pallas import tpu as pltpu
from jax.sharding import PartitionSpec as P

ITER_C = 4
ITER_A = 8
META = 8
DENSE_LIMIT = 1024
OFF = -1e30
BF = jnp.bfloat16
F32 = jnp.float32
VMEM = pl.BlockSpec(memory_space=pltpu.VMEM)
SMEM = pl.BlockSpec(memory_space=pltpu.SMEM)
HIGHEST = lax.Precision.HIGHEST
PARAMS = pltpu.CompilerParams(vmem_limit_bytes=16 << 20)


def dot(a, b, ca, cb, precision=None):
    return lax.dot_general(a, b, (((ca,), (cb,)), ((), ())), precision=precision, preferred_element_type=F32)


def split(x):
    high = x.astype(BF)
    return high, (x - high.astype(F32)).astype(BF)


def pack_kernel(foot_ref, rec_ref, owner_ref, pick_ref, traces_ref, out_ref):
    tiles = out_ref.shape[0]
    slots = foot_ref.shape[1]
    active = traces_ref.shape[0] // 8
    foot = foot_ref[...]
    both = dot(foot, jnp.concatenate([foot, rec_ref[...]], axis=1), 0, 0)
    gram, drive = both[:, :slots], both[:, slots:]
    bound = jnp.sum(jnp.abs(gram), axis=0, keepdims=True)
    high = bound.astype(BF).astype(F32)
    middle = (bound - high).astype(BF).astype(F32)
    low = bound - high - middle
    named = [high, middle, low, owner_ref[...].astype(F32), pick_ref[...].astype(F32)]
    rest = jnp.zeros((META - len(named), slots), F32)
    tail = jnp.concatenate([traces_ref[:active, :]] + named + [rest], axis=0).astype(BF)
    gram = gram.astype(BF)
    drive = drive.astype(BF)
    for tile in range(tiles):
        out_ref[tile, 0:slots, :] = gram
        out_ref[tile, slots : 2 * slots, :] = drive
        out_ref[tile, 2 * slots : 2 * slots + active + META, :] = tail


def gathered_parts(block, slots, active):
    gram = block[:slots]
    drive = block[slots : 2 * slots]
    tail = block[2 * slots :].astype(F32)
    meta = tail[active : active + META]
    return gram, drive, tail[:active], meta


def trace_kernel(tile_ref, got_ref, owner_ref, pick_ref, traces_ref, new_ref, own_ref, cur_ref):
    tiles = got_ref.shape[0]
    slots = got_ref.shape[2]
    frames = traces_ref.shape[1]
    active = traces_ref.shape[0] // 8
    count = tiles * active
    me = tile_ref[0]
    row = lax.broadcasted_iota(jnp.int32, (count, slots), 0).astype(F32)
    picks, bounds, mixed, drives = [], None, [], []
    for tile in range(tiles):
        gram, drive, first, meta = gathered_parts(got_ref[tile], slots, active)
        cur_ref[tile * active : (tile + 1) * active, :] = first
        hit = row == meta[3:4] * float(active) + meta[4:5]
        bound = jnp.where(hit, meta[0:1] + meta[1:2] + meta[2:3], 0.0)
        bounds = bound if bounds is None else bounds + bound
        pick = jnp.where(hit, 1.0, 0.0).astype(BF)
        picks.append(pick)
        drives.append(drive)
        mixed.append(dot(pick, gram, 1, 0))
    pick = jnp.concatenate(picks, axis=1)
    mixed = jnp.concatenate(mixed, axis=1)
    mixed = jnp.concatenate(split(mixed), axis=0)
    whole = dot(mixed, pick, 1, 1)
    whole = whole[:count] + whole[count:]
    pull = dot(pick, jnp.concatenate(drives, axis=0), 1, 0)
    scale = 1.0 / (1.0 + jnp.sum(bounds, axis=1, keepdims=True))
    whole = jnp.concatenate(split(whole), axis=0)
    at = pl.multiple_of(me * active, 8)
    cur_ref[pl.ds(at, active), :] = traces_ref[:active, :]
    current = cur_ref[...]
    for _ in range(ITER_C):
        push = dot(whole, jnp.concatenate(split(current), axis=1), 1, 0)
        push = push[:, :frames] + push[:, frames:]
        push = push[:count] + push[count:]
        current = jnp.maximum(current - (push - pull) * scale, 0.0)
    cur_ref[...] = current
    new_ref[:active, :] = cur_ref[pl.ds(at, active), :]
    new_ref[active:, :] = jnp.maximum(traces_ref[active:, :], 0.0)
    own = jnp.where(row == (owner_ref[...] * active + pick_ref[...]).astype(F32), 1.0, 0.0)
    own_ref[...] = dot(own, current, 0, 0, HIGHEST)


def trace_steps_wide(got, owner, pick, traces, me):
    tiles, _, slots = got.shape
    active = traces.shape[0] // 8
    frames = traces.shape[1]
    gram, drive, first, meta = jax.vmap(lambda b: gathered_parts(b, slots, active))(got)
    index = (meta[:, 3] * active + meta[:, 4]).astype(jnp.int32).reshape(-1)
    bound = jax.ops.segment_sum((meta[:, 0] + meta[:, 1] + meta[:, 2]).reshape(-1), index, num_segments=tiles * active)
    scale = (1.0 / (1.0 + bound))[:, None]
    current = first.reshape(tiles * active, frames)
    current = lax.dynamic_update_slice(current, traces[:active], (me * active, 0))

    def step(_, current):
        taken = jnp.take(current, index, axis=0).reshape(tiles, slots, frames)
        terms = jnp.einsum("tkj,tjf->tkf", gram.astype(F32), taken, precision=HIGHEST) - drive.astype(F32)
        total = jax.ops.segment_sum(terms.reshape(-1, frames), index, num_segments=tiles * active)
        return jnp.maximum(current - total * scale, 0.0)

    current = lax.fori_loop(0, ITER_C, step, current)
    mine = lax.dynamic_slice(current, (me * active, 0), (active, frames))
    new = jnp.concatenate([mine, jnp.maximum(traces[active:], 0.0)], axis=0)
    own = jnp.take(current, owner[0] * active + pick[0], axis=0)
    return new, own


def line_up_kernel(spot_ref, *refs):
    parts, out_ref = refs[:-1], refs[-1]
    for offset, part in enumerate(parts):
        out_ref[spot_ref[0] ^ offset] = part[...]


def sweep_kernel(foot_ref, rec_ref, own_ref, out_ref, cur_ref, add_ref):
    lanes, slots, _ = own_ref.shape
    own = jnp.concatenate([own_ref[lane] for lane in range(lanes)], axis=1)
    rec = jnp.concatenate([rec_ref[lane] for lane in range(lanes)], axis=1)
    gram = dot(own, own, 1, 1, HIGHEST)
    step = 1.0 / (1.0 + jnp.sum(jnp.abs(gram), axis=0, keepdims=True))
    data = dot(rec, own.astype(BF), 1, 1)
    foot = foot_ref[...].astype(F32)
    add_ref[...] = jnp.where(foot > 0, data * step, OFF)
    cur_ref[...] = foot
    mix = jnp.concatenate(split(gram * step), axis=1)
    mix = jnp.concatenate([mix, mix], axis=0)

    @pl.loop(0, ITER_A)
    def _(_):
        now = cur_ref[...]
        moved = dot(jnp.concatenate(split(now), axis=1), mix, 1, 0)
        cur_ref[...] = jnp.maximum(now - (moved[:, :slots] + moved[:, slots:]) + add_ref[...], 0.0)

    out_ref[...] = cur_ref[...].astype(BF)


def body(recording, footprints, slot_owner, slot_pick, traces):
    tiles = lax.axis_size("tile")
    lanes = lax.axis_size("frame")
    voxels, slots = footprints.shape
    owned, frames = traces.shape
    active = owned // 8
    me = lax.axis_index("tile").astype(jnp.int32)[None]
    spot = lax.axis_index("frame").astype(jnp.int32)[None]
    owner = slot_owner.reshape(1, slots)
    pick = slot_pick.reshape(1, slots)
    rows = 2 * slots + active + META

    def swap(value, bit):
        return lax.ppermute(value, "frame", [(i, i ^ bit) for i in range(lanes)])

    packed = pl.pallas_call(
        pack_kernel,
        out_shape=jax.ShapeDtypeStruct((tiles, rows, slots), BF),
        in_specs=[VMEM] * 5,
        out_specs=VMEM,
        compiler_params=PARAMS,
        name="pack",
    )(footprints, recording, owner, pick, traces)
    got = lax.all_to_all(packed, "tile", split_axis=0, concat_axis=0, tiled=True)
    blocks = [recording]
    bit = 1
    while bit < lanes:
        blocks = blocks + [swap(block, bit) for block in blocks]
        bit = 2 * bit
    lined = pl.pallas_call(
        line_up_kernel,
        out_shape=jax.ShapeDtypeStruct((lanes, voxels, frames), BF),
        in_specs=[SMEM] + [VMEM] * lanes,
        out_specs=VMEM,
        compiler_params=PARAMS,
        name="line_up",
    )(spot, *blocks)
    if tiles * active <= DENSE_LIMIT:
        new_traces, own = pl.pallas_call(
            trace_kernel,
            out_shape=(jax.ShapeDtypeStruct((owned, frames), F32), jax.ShapeDtypeStruct((slots, frames), F32)),
            in_specs=[SMEM] + [VMEM] * 4,
            out_specs=(VMEM, VMEM),
            scratch_shapes=[pltpu.VMEM((tiles * active, frames), F32)],
            compiler_params=PARAMS,
            name="traces",
        )(me, got, owner, pick, traces)
    else:
        new_traces, own = trace_steps_wide(got, owner, pick, traces, me[0])
    every = lax.all_gather(own, "frame", axis=0)
    updated = pl.pallas_call(
        sweep_kernel,
        out_shape=jax.ShapeDtypeStruct((voxels, slots), BF),
        in_specs=[VMEM] * 3,
        out_specs=VMEM,
        scratch_shapes=[pltpu.VMEM((voxels, slots), F32)] * 2,
        compiler_params=PARAMS,
        name="sweeps",
    )(footprints, lined, every)
    return (new_traces, updated)


def solution(mesh):
    in_specs = (P("tile", "frame"), P("tile", None), P("tile", None), P("tile"), P("tile", "frame"))
    out_specs = (P("tile", "frame"), P("tile", None))
    return jax.shard_map(body, mesh=mesh, in_specs=in_specs, out_specs=out_specs, check_vma=False)
```

```python
import jax
import jax.numpy as jnp
from jax import lax
from jax.experimental import pallas as pl
from jax.experimental.pallas import tpu as pltpu
from jax.sharding import PartitionSpec as P

ITER_C = 4
ITER_A = 8
META = 8
DENSE_LIMIT = 1024
OFF = -1e30
BF = jnp.bfloat16
F32 = jnp.float32
VMEM = pl.BlockSpec(memory_space=pltpu.VMEM)
SMEM = pl.BlockSpec(memory_space=pltpu.SMEM)
HBM = pl.BlockSpec(memory_space=pltpu.MemorySpace.HBM)
HIGHEST = lax.Precision.HIGHEST
PARAMS = pltpu.CompilerParams(vmem_limit_bytes=16 << 20)


def dot(a, b, ca, cb, precision=None):
    return lax.dot_general(a, b, (((ca,), (cb,)), ((), ())), precision=precision, preferred_element_type=F32)


def split(x):
    high = x.astype(BF)
    return high, (x - high.astype(F32)).astype(BF)


def start(sems, pairs):
    copies = [pltpu.make_async_copy(source, target, sems.at[i]) for i, (source, target) in enumerate(pairs)]
    for copy in copies:
        copy.start()
    return copies


def pack_kernel(core_ref, foot_hbm, rec_hbm, owner_hbm, pick_hbm, traces_hbm, out_ref, foot_ref, rec_ref, owner_ref, pick_ref, traces_ref, gram_ref, sems):
    tiles = out_ref.shape[0]
    slots = foot_ref.shape[1]
    half = slots // 2
    active = traces_ref.shape[0]
    copies = start(
        sems,
        [
            (foot_hbm, foot_ref),
            (rec_hbm, rec_ref),
            (owner_hbm, owner_ref),
            (pick_hbm, pick_ref),
            (traces_hbm.at[pl.ds(0, active), :], traces_ref),
        ],
    )
    for copy in copies:
        copy.wait()
    foot = foot_ref[...]
    both = dot(foot, jnp.concatenate([foot, rec_ref[...]], axis=1), 0, 0)
    gram, drive = both[:, :slots], both[:, slots:].astype(BF)
    bound = jnp.sum(jnp.abs(gram), axis=0, keepdims=True)
    high = bound.astype(BF).astype(F32)
    middle = (bound - high).astype(BF).astype(F32)
    low = bound - high - middle
    named = [high, middle, low, owner_ref[...].astype(F32), pick_ref[...].astype(F32)]
    rest = jnp.zeros((META - len(named), slots), F32)
    tail = jnp.concatenate([traces_ref[...]] + named + [rest], axis=0).astype(BF)
    gram_ref[...] = gram.astype(BF)
    gram = gram_ref[pl.ds(pl.multiple_of(core_ref[0] * half, 16), half), :]
    for tile in range(tiles):
        out_ref[tile, 0:half, :] = gram
        out_ref[tile, half : half + slots, :] = drive
        out_ref[tile, half + slots : half + slots + active + META, :] = tail


def meta_of(tail, active):
    meta = tail[active : active + META]
    return meta[0:1] + meta[1:2] + meta[2:3], meta[3:4] * float(active) + meta[4:5]


def begin_kernel(tile_ref, got_ref, traces_hbm, pick_ref, pull_ref, scale_ref, cur_ref, sems):
    tiles, rows, slots = got_ref.shape
    half = slots // 2
    active = rows - half - slots - META
    count = tiles * active
    drives, bounds = [], None
    row = lax.broadcasted_iota(jnp.int32, (count, slots), 0).astype(F32)
    for tile in range(tiles):
        tail = got_ref[tile, half + slots :, :].astype(F32)
        cur_ref[tile * active : (tile + 1) * active, :] = tail[:active]
        bound, index = meta_of(tail, active)
        hit = row == index
        bound = jnp.where(hit, bound, 0.0)
        bounds = bound if bounds is None else bounds + bound
        pick_ref[tile] = jnp.where(hit, 1.0, 0.0).astype(BF)
        drives.append(got_ref[tile, half : half + slots, :])
    at = pl.multiple_of(tile_ref[0] * active, 8)
    copies = start(sems, [(traces_hbm.at[pl.ds(0, active), :], cur_ref.at[pl.ds(at, active), :])])
    pick = jnp.concatenate([pick_ref[tile] for tile in range(tiles)], axis=1)
    pull_ref[...] = dot(pick, jnp.concatenate(drives, axis=0), 1, 0)
    scale_ref[...] = jnp.broadcast_to(1.0 / (1.0 + jnp.sum(bounds, axis=1, keepdims=True)), scale_ref.shape)
    for copy in copies:
        copy.wait()


def trace_kernel(core_ref, tile_ref, got_ref, far_ref, pick_ref, pull_ref, scale_ref, cur_ref, new_ref, own_ref, gram_ref):
    tiles, count, slots = pick_ref.shape
    half = slots // 2
    frames = cur_ref.shape[1]
    here = pl.multiple_of(core_ref[0] * half, 16)
    there = pl.multiple_of((1 - core_ref[0]) * half, 16)
    mixed = []
    for tile in range(tiles):
        gram_ref[tile, pl.ds(here, half), :] = got_ref[tile, :half, :]
        gram_ref[tile, pl.ds(there, half), :] = far_ref[tile, :half, :]
        mixed.append(dot(pick_ref[tile], gram_ref[tile], 1, 0))
    pick = jnp.concatenate([pick_ref[tile] for tile in range(tiles)], axis=1)
    mixed = jnp.concatenate(split(jnp.concatenate(mixed, axis=1)), axis=0)
    whole = dot(mixed, pick, 1, 1)
    whole = jnp.concatenate(split(whole[:count] + whole[count:]), axis=0)
    pull, scale, current = pull_ref[...], scale_ref[...], cur_ref[...]
    for _ in range(ITER_C):
        push = dot(whole, jnp.concatenate(split(current), axis=1), 1, 0)
        push = push[:, :frames] + push[:, frames:]
        current = jnp.maximum(current - (push[:count] + push[count:] - pull) * scale, 0.0)
    new_ref[...] = current
    high, low = split(current)
    last = (current - high.astype(F32) - low.astype(F32)).astype(BF)
    own = dot(pick_ref[tile_ref[0]], jnp.concatenate([high, low, last], axis=1), 0, 0)
    own_ref[...] = own[:, :frames] + own[:, frames : 2 * frames] + own[:, 2 * frames :]


def trace_steps_wide(got, far, owner, pick, traces, me, core):
    tiles, _, slots = got.shape
    half = slots // 2
    active = traces.shape[0] // 8
    frames = traces.shape[1]
    mine, theirs = got[:, :half].astype(F32), far[:, :half].astype(F32)
    gram = jnp.where(core == 0, jnp.concatenate([mine, theirs], axis=1), jnp.concatenate([theirs, mine], axis=1))
    drive = got[:, half : half + slots].astype(F32)
    tail = got[:, half + slots :].astype(F32)
    bound, index = jax.vmap(lambda t: meta_of(t, active))(tail)
    index = index.astype(jnp.int32).reshape(-1)
    bound = jax.ops.segment_sum(bound.reshape(-1), index, num_segments=tiles * active)
    scale = (1.0 / (1.0 + bound))[:, None]
    current = tail[:, :active].reshape(tiles * active, frames)
    current = lax.dynamic_update_slice(current, traces[:active], (me * active, 0))

    def step(_, current):
        taken = jnp.take(current, index, axis=0).reshape(tiles, slots, frames)
        terms = jnp.einsum("tkj,tjf->tkf", gram, taken, precision=HIGHEST) - drive
        total = jax.ops.segment_sum(terms.reshape(-1, frames), index, num_segments=tiles * active)
        return jnp.maximum(current - total * scale, 0.0)

    current = lax.fori_loop(0, ITER_C, step, current)
    return current, jnp.take(current, owner[0] * active + pick[0], axis=0)


def line_up_kernel(spot_ref, *refs):
    parts, out_ref = refs[:-1], refs[-1]
    for offset, part in enumerate(parts):
        out_ref[spot_ref[0] ^ offset] = part[...]


def sweep_kernel(tile_ref, foot_hbm, traces_hbm, cur_ref, rec_ref, own_ref, out_ref, new_hbm, foot_ref, traces_ref, now_ref, add_ref, sems):
    lanes, slots, _ = own_ref.shape
    owned = traces_ref.shape[0]
    active = owned // 8
    at = pl.multiple_of(tile_ref[0] * active, 8)
    copies = start(
        sems,
        [
            (foot_hbm, foot_ref),
            (traces_hbm.at[pl.ds(active, owned - active), :], traces_ref.at[pl.ds(active, owned - active), :]),
        ],
    )
    own = jnp.concatenate([own_ref[lane] for lane in range(lanes)], axis=1)
    rec = jnp.concatenate([rec_ref[lane] for lane in range(lanes)], axis=1)
    gram = dot(own, own, 1, 1, HIGHEST)
    step = 1.0 / (1.0 + jnp.sum(jnp.abs(gram), axis=0, keepdims=True))
    data = dot(rec, own.astype(BF), 1, 1)
    mix = jnp.concatenate(split(gram * step), axis=1)
    mix = jnp.concatenate([mix, mix], axis=0)
    for copy in copies:
        copy.wait()
    traces_ref[:active, :] = cur_ref[pl.ds(at, active), :]
    traces_ref[active:, :] = jnp.maximum(traces_ref[active:, :], 0.0)
    last = pltpu.make_async_copy(traces_ref, new_hbm, sems.at[0])
    last.start()
    foot = foot_ref[...].astype(F32)
    add_ref[...] = jnp.where(foot > 0, data * step, OFF)
    now_ref[...] = foot

    @pl.loop(0, ITER_A)
    def _(_):
        now = now_ref[...]
        moved = dot(jnp.concatenate(split(now), axis=1), mix, 1, 0)
        now_ref[...] = jnp.maximum(now - (moved[:, :slots] + moved[:, slots:]) + add_ref[...], 0.0)

    out_ref[...] = now_ref[...].astype(BF)
    last.wait()


def body(recording, footprints, slot_owner, slot_pick, traces):
    tiles = lax.axis_size("tile")
    lanes = lax.axis_size("frame")
    voxels, slots = footprints.shape
    owned, frames = traces.shape
    active = owned // 8
    half = slots // 2
    count = tiles * active
    me = lax.axis_index("tile").astype(jnp.int32)[None]
    spot = lax.axis_index("frame").astype(jnp.int32)[None]
    core = spot & 1
    owner = slot_owner.reshape(1, slots)
    pick = slot_pick.reshape(1, slots)
    rows = half + slots + active + META

    def swap(value, bit):
        return lax.ppermute(value, "frame", [(i, i ^ bit) for i in range(lanes)])

    def shape(dims, dtype=F32):
        return jax.ShapeDtypeStruct(dims, dtype)

    packed = pl.pallas_call(
        pack_kernel,
        out_shape=shape((tiles, rows, slots), BF),
        in_specs=[SMEM] + [HBM] * 5,
        out_specs=VMEM,
        scratch_shapes=[
            pltpu.VMEM((voxels, slots), BF),
            pltpu.VMEM((voxels, frames), BF),
            pltpu.VMEM((1, slots), jnp.int32),
            pltpu.VMEM((1, slots), jnp.int32),
            pltpu.VMEM((active, frames), F32),
            pltpu.VMEM((slots, slots), BF),
            pltpu.SemaphoreType.DMA((5,)),
        ],
        name="pack",
    )(core, footprints, recording, owner, pick, traces)
    got = lax.all_to_all(packed, "tile", split_axis=0, concat_axis=0, tiled=True)

    blocks = [recording] + [swap(recording, bit) for bit in range(2, lanes, 2)]
    blocks = [part for block in blocks for part in (block, swap(block, 1))]
    lined = pl.pallas_call(
        line_up_kernel,
        out_shape=shape((lanes, voxels, frames), BF),
        in_specs=[SMEM] + [VMEM] * lanes,
        out_specs=VMEM,
        compiler_params=PARAMS,
        name="line_up",
    )(spot, *blocks)
    got, lined = lax.optimization_barrier((got, lined))
    far = swap(got, 1)
    if count <= DENSE_LIMIT:
        begun = pl.pallas_call(
            begin_kernel,
            out_shape=(shape((tiles, count, slots), BF),) + (shape((count, frames)),) * 3,
            in_specs=[SMEM, VMEM, HBM],
            out_specs=(VMEM,) * 4,
            scratch_shapes=[pltpu.SemaphoreType.DMA((1,))],
            compiler_params=PARAMS,
            name="begin",
        )(me, got, traces)
        current, own = pl.pallas_call(
            trace_kernel,
            out_shape=(shape((count, frames)), shape((slots, frames))),
            in_specs=[SMEM] * 2 + [VMEM] * 6,
            out_specs=(VMEM,) * 2,
            scratch_shapes=[pltpu.VMEM((tiles, slots, slots), BF)],
            compiler_params=PARAMS,
            name="traces",
        )(core, me, got, far, *begun)
    else:
        current, own = trace_steps_wide(got, far, owner, pick, traces, me[0], core[0])
    every = lax.all_gather(own, "frame", axis=0)
    updated, new_traces = pl.pallas_call(
        sweep_kernel,
        out_shape=(shape((voxels, slots), BF), shape((owned, frames))),
        in_specs=[SMEM] + [HBM] * 2 + [VMEM] * 3,
        out_specs=(VMEM, HBM),
        scratch_shapes=[
            pltpu.VMEM((voxels, slots), BF),
            pltpu.VMEM((owned, frames), F32),
            pltpu.VMEM((voxels, slots), F32),
            pltpu.VMEM((voxels, slots), F32),
            pltpu.SemaphoreType.DMA((2,)),
        ],
        compiler_params=PARAMS,
        name="sweeps",
    )(me, footprints, traces, current, lined, every)
    return (new_traces, updated)


def solution(mesh):
    in_specs = (P("tile", "frame"), P("tile", None), P("tile", None), P("tile"), P("tile", "frame"))
    out_specs = (P("tile", "frame"), P("tile", None))
    return jax.shard_map(body, mesh=mesh, in_specs=in_specs, out_specs=out_specs, check_vma=False)
```

```python
import jax
import jax.numpy as jnp
from jax import lax
from jax.experimental import pallas as pl
from jax.experimental.pallas import tpu as pltpu
from jax.sharding import PartitionSpec as P

ITER_C = 4
ITER_A = 8
META = 8
BLOCKS = 4
DENSE_LIMIT = 1024
OFF = -1e30
BF = jnp.bfloat16
F32 = jnp.float32
VMEM = pl.BlockSpec(memory_space=pltpu.VMEM)
SMEM = pl.BlockSpec(memory_space=pltpu.SMEM)
HBM = pl.BlockSpec(memory_space=pltpu.MemorySpace.HBM)
HIGHEST = lax.Precision.HIGHEST
PARAMS = pltpu.CompilerParams(vmem_limit_bytes=16 << 20)


def dot(a, b, ca, cb, precision=None):
    return lax.dot_general(a, b, (((ca,), (cb,)), ((), ())), precision=precision, preferred_element_type=F32)


def split(x):
    high = x.astype(BF)
    return high, (x - high.astype(F32)).astype(BF)


def start(sems, pairs):
    copies = [pltpu.make_async_copy(source, target, sems.at[i]) for i, (source, target) in enumerate(pairs)]
    for copy in copies:
        copy.start()
    return copies


def pack_kernel(core_ref, foot_hbm, rec_hbm, owner_hbm, pick_hbm, traces_hbm, out_ref, foot_ref, rec_ref, owner_ref, pick_ref, traces_ref, gram_ref, sems):
    tiles = out_ref.shape[0]
    slots = foot_ref.shape[1]
    frames = rec_ref.shape[1]
    half = slots // 2
    active = traces_ref.shape[0]
    copies = start(
        sems,
        [
            (foot_hbm, foot_ref),
            (rec_hbm, rec_ref),
            (owner_hbm, owner_ref),
            (pick_hbm, pick_ref),
            (traces_hbm.at[pl.ds(0, active), :], traces_ref),
        ],
    )
    for copy in copies:
        copy.wait()
    foot = foot_ref[...]
    both = dot(foot, jnp.concatenate([foot, rec_ref[...]], axis=1), 0, 0)
    gram, drive = both[:, :slots], both[:, slots:].T.astype(BF)
    bound = jnp.sum(jnp.abs(gram), axis=0, keepdims=True)
    high = bound.astype(BF).astype(F32)
    middle = (bound - high).astype(BF).astype(F32)
    low = bound - high - middle
    named = [high, middle, low, owner_ref[...].astype(F32), pick_ref[...].astype(F32)]
    rest = jnp.zeros((META - len(named), slots), F32)
    tail = jnp.concatenate([traces_ref[...]] + named + [rest], axis=0).astype(BF)
    gram_ref[...] = gram.astype(BF)
    gram = gram_ref[pl.ds(pl.multiple_of(core_ref[0] * half, 16), half), :]
    for tile in range(tiles):
        out_ref[tile, 0:half, :] = gram
        out_ref[tile, half : half + frames, :] = drive
        out_ref[tile, half + frames : half + frames + active + META, :] = tail


def index_of(tail, active):
    meta = tail[active : active + META]
    return meta[3:4] * float(active) + meta[4:5]


def begin_kernel(tile_ref, got_ref, traces_hbm, pick_ref, pull_ref, scale_ref, cur_ref, first_ref, sems):
    tiles, rows, slots = got_ref.shape
    frames = cur_ref.shape[0]
    half = slots // 2
    active = rows - half - frames - META
    count = tiles * active
    row = lax.broadcasted_iota(jnp.int32, (count, slots), 0).astype(F32)
    for tile in range(tiles):
        tail = got_ref[tile, half + frames :, :].astype(F32)
        first_ref[tile * active : (tile + 1) * active, :] = tail[:active]
        pick_ref[tile] = jnp.where(row == index_of(tail, active), 1.0, 0.0).astype(BF)
    at = pl.multiple_of(tile_ref[0] * active, 8)
    copies = start(sems, [(traces_hbm.at[pl.ds(0, active), :], first_ref.at[pl.ds(at, active), :])])
    pick = jnp.concatenate([pick_ref[tile] for tile in range(tiles)], axis=1)
    parts = jnp.concatenate([got_ref[tile, half:, :] for tile in range(tiles)], axis=1)
    sums = dot(parts, pick, 1, 1)
    pull_ref[...] = sums[:frames]
    bound = sums[frames + active : frames + active + META]
    scale_ref[...] = jnp.broadcast_to(1.0 / (1.0 + bound[0:1] + bound[1:2] + bound[2:3]), scale_ref.shape)
    for copy in copies:
        copy.wait()
    cur_ref[...] = first_ref[...].T


def trace_kernel(core_ref, tile_ref, got_ref, far_ref, pick_ref, pull_ref, scale_ref, cur_ref, new_ref, own_ref, gram_ref):
    tiles, count, slots = pick_ref.shape
    half = slots // 2
    frames = cur_ref.shape[0]
    here = pl.multiple_of(core_ref[0] * half, 16)
    there = pl.multiple_of((1 - core_ref[0]) * half, 16)
    mixed = []
    for tile in range(tiles):
        gram_ref[tile, pl.ds(here, half), :] = got_ref[tile, :half, :]
        gram_ref[tile, pl.ds(there, half), :] = far_ref[tile, :half, :]
        mixed.append(dot(pick_ref[tile], gram_ref[tile], 1, 0))
    pick = jnp.concatenate([pick_ref[tile] for tile in range(tiles)], axis=1)
    mixed = jnp.concatenate(split(jnp.concatenate(mixed, axis=1)), axis=0)
    whole = dot(mixed, pick, 1, 1)
    whole_high, whole_low = split(whole[:count] + whole[count:])
    pull, scale, current = pull_ref[...], scale_ref[0:1, :], cur_ref[...]
    for _ in range(ITER_C):
        high, low = split(current)
        push = dot(jnp.concatenate([high, low], axis=0), whole_high, 1, 0)
        push = push[:frames] + push[frames:] + dot(high, whole_low, 1, 0)
        current = jnp.maximum(current - (push - pull) * scale, 0.0)
    new_ref[...] = current
    own_ref[...] = dot(current.astype(BF), pick_ref[tile_ref[0]], 1, 0).astype(BF)


def trace_steps_wide(got, far, owner, pick, traces, me, core):
    tiles, _, slots = got.shape
    half = slots // 2
    active = traces.shape[0] // 8
    frames = traces.shape[1]
    mine, theirs = got[:, :half].astype(F32), far[:, :half].astype(F32)
    gram = jnp.where(core == 0, jnp.concatenate([mine, theirs], axis=1), jnp.concatenate([theirs, mine], axis=1))
    drive = got[:, half : half + frames].astype(F32).transpose(0, 2, 1)
    tail = got[:, half + frames :].astype(F32)
    index = jax.vmap(lambda t: index_of(t, active))(tail).astype(jnp.int32).reshape(-1)
    bound = jnp.sum(tail[:, active : active + 3], axis=1).reshape(-1)
    bound = jax.ops.segment_sum(bound, index, num_segments=tiles * active)
    scale = (1.0 / (1.0 + bound))[:, None]
    current = tail[:, :active].reshape(tiles * active, frames)
    current = lax.dynamic_update_slice(current, traces[:active], (me * active, 0))

    def step(_, current):
        taken = jnp.take(current, index, axis=0).reshape(tiles, slots, frames)
        terms = jnp.einsum("tkj,tjf->tkf", gram, taken, precision=HIGHEST) - drive
        total = jax.ops.segment_sum(terms.reshape(-1, frames), index, num_segments=tiles * active)
        return jnp.maximum(current - total * scale, 0.0)

    current = lax.fori_loop(0, ITER_C, step, current)
    own = jnp.take(current, owner[0] * active + pick[0], axis=0)
    mine = lax.dynamic_slice(current, (me * active, 0), (active, frames))
    return mine.T, own.T.astype(BF)


def line_up_kernel(spot_ref, *refs):
    parts, out_ref = refs[:-1], refs[-1]
    for offset, part in enumerate(parts):
        out_ref[spot_ref[0] ^ offset] = part[...]


def sweep_kernel(tile_ref, foot_ref, traces_ref, cur_ref, rec_ref, own_ref, out_hbm, new_hbm, all_ref, out_ref, new_ref, now_ref, add_ref, sems):
    lanes = rec_ref.shape[0]
    owned = new_ref.shape[0]
    voxels, slots = foot_ref.shape
    active = owned // 8
    count = cur_ref.shape[1]
    all_ref[...] = cur_ref[...].T
    at = pl.multiple_of(tile_ref[0] * active if count > active else 0, 8)
    new_ref[:active, :] = all_ref[pl.ds(at, active), :]
    new_ref[active:, :] = jnp.maximum(traces_ref[active:, :], 0.0)
    copies = start(sems, [(new_ref, new_hbm)])
    own = own_ref[...]
    gram = dot(own, own, 0, 0)
    data = dot(jnp.concatenate([rec_ref[lane] for lane in range(lanes)], axis=1), own, 1, 0)
    step = 1.0 / (1.0 + jnp.sum(jnp.abs(gram), axis=0, keepdims=True))
    mix = jnp.concatenate(split(gram * step), axis=1)
    mix = jnp.concatenate([mix, mix], axis=0)
    foot = foot_ref[...].astype(F32)
    add_ref[...] = jnp.where(foot > 0, data * step, OFF)
    now_ref[...] = foot

    def swept(part):
        now = now_ref[part, :]
        moved = dot(jnp.concatenate(split(now), axis=1), mix, 1, 0)
        return jnp.maximum(now - (moved[:, :slots] + moved[:, slots:]) + add_ref[part, :], 0.0)

    for _ in range(ITER_A - 1):
        now_ref[...] = swept(slice(None))
    size = voxels // BLOCKS
    for block in range(BLOCKS):
        out_ref[block * size : (block + 1) * size, :] = swept(slice(block * size, (block + 1) * size)).astype(BF)
        part = pl.ds(block * size, size)
        copies += start(sems.at[pl.ds(1 + block, 1)], [(out_ref.at[part, :], out_hbm.at[part, :])])
    for copy in copies:
        copy.wait()


def body(recording, footprints, slot_owner, slot_pick, traces):
    tiles = lax.axis_size("tile")
    lanes = lax.axis_size("frame")
    voxels, slots = footprints.shape
    owned, frames = traces.shape
    active = owned // 8
    half = slots // 2
    count = tiles * active
    me = lax.axis_index("tile").astype(jnp.int32)[None]
    spot = lax.axis_index("frame").astype(jnp.int32)[None]
    core = spot & 1
    owner = slot_owner.reshape(1, slots)
    pick = slot_pick.reshape(1, slots)
    rows = half + frames + active + META

    def swap(value, bit):
        return lax.ppermute(value, "frame", [(i, i ^ bit) for i in range(lanes)])

    def shape(dims, dtype=F32):
        return jax.ShapeDtypeStruct(dims, dtype)

    packed = pl.pallas_call(
        pack_kernel,
        out_shape=shape((tiles, rows, slots), BF),
        in_specs=[SMEM] + [HBM] * 5,
        out_specs=VMEM,
        scratch_shapes=[
            pltpu.VMEM((voxels, slots), BF),
            pltpu.VMEM((voxels, frames), BF),
            pltpu.VMEM((1, slots), jnp.int32),
            pltpu.VMEM((1, slots), jnp.int32),
            pltpu.VMEM((active, frames), F32),
            pltpu.VMEM((slots, slots), BF),
            pltpu.SemaphoreType.DMA((5,)),
        ],
        name="pack",
    )(core, footprints, recording, owner, pick, traces)
    got = lax.all_to_all(packed, "tile", split_axis=0, concat_axis=0, tiled=True)

    blocks = [recording] + [swap(recording, bit) for bit in range(2, lanes, 2)]
    blocks = [part for block in blocks for part in (block, swap(block, 1))]
    lined = pl.pallas_call(
        line_up_kernel,
        out_shape=shape((lanes, voxels, frames), BF),
        in_specs=[SMEM] + [VMEM] * lanes,
        out_specs=VMEM,
        compiler_params=PARAMS,
        name="line_up",
    )(spot, *blocks)
    got, lined = lax.optimization_barrier((got, lined))
    far = swap(got, 1)
    if count <= DENSE_LIMIT:
        begun = pl.pallas_call(
            begin_kernel,
            out_shape=(
                shape((tiles, count, slots), BF),
                shape((frames, count)),
                shape((8, count)),
                shape((frames, count)),
            ),
            in_specs=[SMEM, VMEM, HBM],
            out_specs=(VMEM,) * 4,
            scratch_shapes=[pltpu.VMEM((count, frames), F32), pltpu.SemaphoreType.DMA((1,))],
            compiler_params=PARAMS,
            name="begin",
        )(me, got, traces)
        current, own = pl.pallas_call(
            trace_kernel,
            out_shape=(shape((frames, count)), shape((frames, slots), BF)),
            in_specs=[SMEM] * 2 + [VMEM] * 6,
            out_specs=(VMEM,) * 2,
            scratch_shapes=[pltpu.VMEM((tiles, slots, slots), BF)],
            compiler_params=PARAMS,
            name="traces",
        )(core, me, got, far, *begun)
    else:
        current, own = trace_steps_wide(got, far, owner, pick, traces, me[0], core[0])
    every = lax.all_gather(own, "frame", axis=0, tiled=True)
    updated, new_traces = pl.pallas_call(
        sweep_kernel,
        out_shape=(shape((voxels, slots), BF), shape((owned, frames))),
        in_specs=[SMEM] + [VMEM] * 5,
        out_specs=(HBM, HBM),
        scratch_shapes=[
            pltpu.VMEM(current.shape[::-1], F32),
            pltpu.VMEM((voxels, slots), BF),
            pltpu.VMEM((owned, frames), F32),
            pltpu.VMEM((voxels, slots), F32),
            pltpu.VMEM((voxels, slots), F32),
            pltpu.SemaphoreType.DMA((1 + BLOCKS,)),
        ],
        compiler_params=PARAMS,
        name="sweeps",
    )(me, footprints, traces, current, lined, every)
    return (new_traces, updated)


def solution(mesh):
    in_specs = (P("tile", "frame"), P("tile", None), P("tile", None), P("tile"), P("tile", "frame"))
    out_specs = (P("tile", "frame"), P("tile", None))
    return jax.shard_map(body, mesh=mesh, in_specs=in_specs, out_specs=out_specs, check_vma=False)
```

```python
import jax
import jax.numpy as jnp
from jax import lax
from jax.experimental import pallas as pl
from jax.experimental.pallas import tpu as pltpu
from jax.sharding import PartitionSpec as P

ITER_C = 4
ITER_A = 8
META = 8
BLOCKS = 4
DENSE_LIMIT = 1024
OFF = -1e30
BF = jnp.bfloat16
F32 = jnp.float32
VMEM = pl.BlockSpec(memory_space=pltpu.VMEM)
SMEM = pl.BlockSpec(memory_space=pltpu.SMEM)
HBM = pl.BlockSpec(memory_space=pltpu.MemorySpace.HBM)
HIGHEST = lax.Precision.HIGHEST
PARAMS = pltpu.CompilerParams(vmem_limit_bytes=16 << 20)


def dot(a, b, ca, cb, precision=None):
    return lax.dot_general(a, b, (((ca,), (cb,)), ((), ())), precision=precision, preferred_element_type=F32)


def split(x):
    high = x.astype(BF)
    return high, (x - high.astype(F32)).astype(BF)


def place(source, tiles):
    return (source - tiles // 2) % tiles


def start(sems, pairs):
    copies = [pltpu.make_async_copy(source, target, sems.at[i]) for i, (source, target) in enumerate(pairs)]
    for copy in copies:
        copy.start()
    return copies


def pack_kernel(core_ref, foot_hbm, rec_hbm, owner_hbm, pick_hbm, traces_hbm, out_ref, foot_ref, rec_ref, owner_ref, pick_ref, traces_ref, gram_ref, sems):
    tiles = out_ref.shape[0]
    slots = foot_ref.shape[1]
    frames = rec_ref.shape[1]
    half = slots // 2
    active = traces_ref.shape[0]
    copies = start(
        sems,
        [
            (foot_hbm, foot_ref),
            (rec_hbm, rec_ref),
            (owner_hbm, owner_ref),
            (pick_hbm, pick_ref),
            (traces_hbm.at[pl.ds(0, active), :], traces_ref),
        ],
    )
    for copy in copies:
        copy.wait()
    foot = foot_ref[...]
    both = dot(foot, jnp.concatenate([foot, rec_ref[...]], axis=1), 0, 0)
    gram, drive = both[:, :slots], both[:, slots:].T.astype(BF)
    bound = jnp.sum(jnp.abs(gram), axis=0, keepdims=True)
    high = bound.astype(BF).astype(F32)
    middle = (bound - high).astype(BF).astype(F32)
    low = bound - high - middle
    named = [high, middle, low, owner_ref[...].astype(F32), pick_ref[...].astype(F32)]
    rest = jnp.zeros((META - len(named), slots), F32)
    tail = jnp.concatenate([traces_ref[...]] + named + [rest], axis=0).astype(BF)
    gram_ref[...] = gram.astype(BF)
    gram = gram_ref[pl.ds(pl.multiple_of(core_ref[0] * half, 16), half), :]
    for tile in range(tiles):
        out_ref[tile, 0:half, :] = gram
        out_ref[tile, half : half + frames, :] = drive
        out_ref[tile, half + frames : half + frames + active + META, :] = tail


def index_of(tail, active):
    meta = tail[active : active + META]
    return meta[3:4] * float(active) + meta[4:5]


def begin_kernel(tile_ref, got_ref, traces_hbm, pick_ref, pull_ref, scale_ref, cur_ref, first_ref, sems):
    tiles, rows, slots = got_ref.shape
    frames = cur_ref.shape[0]
    half = slots // 2
    active = rows - half - frames - META
    count = tiles * active
    row = lax.broadcasted_iota(jnp.int32, (count, slots), 0).astype(F32)
    for tile in range(tiles):
        tail = got_ref[place(tile, tiles), half + frames :, :].astype(F32)
        first_ref[tile * active : (tile + 1) * active, :] = tail[:active]
        pick_ref[tile] = jnp.where(row == index_of(tail, active), 1.0, 0.0).astype(BF)
    at = pl.multiple_of(tile_ref[0] * active, 8)
    copies = start(sems, [(traces_hbm.at[pl.ds(0, active), :], first_ref.at[pl.ds(at, active), :])])
    pick = jnp.concatenate([pick_ref[tile] for tile in range(tiles)], axis=1)
    parts = jnp.concatenate([got_ref[place(tile, tiles), half:, :] for tile in range(tiles)], axis=1)
    sums = dot(parts, pick, 1, 1)
    pull_ref[...] = sums[:frames]
    bound = sums[frames + active : frames + active + META]
    scale_ref[...] = jnp.broadcast_to(1.0 / (1.0 + bound[0:1] + bound[1:2] + bound[2:3]), scale_ref.shape)
    for copy in copies:
        copy.wait()
    cur_ref[...] = first_ref[...].T


def trace_kernel(core_ref, tile_ref, got_ref, far_ref, pick_ref, pull_ref, scale_ref, cur_ref, new_ref, own_ref, gram_ref):
    tiles, count, slots = pick_ref.shape
    half = slots // 2
    frames = cur_ref.shape[0]
    here = pl.multiple_of(core_ref[0] * half, 16)
    there = pl.multiple_of((1 - core_ref[0]) * half, 16)
    mixed = []
    for tile in range(tiles):
        gram_ref[tile, pl.ds(here, half), :] = got_ref[place(tile, tiles), :half, :]
        gram_ref[tile, pl.ds(there, half), :] = far_ref[place(tile, tiles), :half, :]
        mixed.append(dot(pick_ref[tile], gram_ref[tile], 1, 0))
    pick = jnp.concatenate([pick_ref[tile] for tile in range(tiles)], axis=1)
    mixed = jnp.concatenate(split(jnp.concatenate(mixed, axis=1)), axis=0)
    whole = dot(mixed, pick, 1, 1)
    whole_high, whole_low = split(whole[:count] + whole[count:])
    pull, scale, current = pull_ref[...], scale_ref[0:1, :], cur_ref[...]
    for _ in range(ITER_C):
        high, low = split(current)
        push = dot(jnp.concatenate([high, low], axis=0), whole_high, 1, 0)
        push = push[:frames] + push[frames:] + dot(high, whole_low, 1, 0)
        current = jnp.maximum(current - (push - pull) * scale, 0.0)
    new_ref[...] = current
    own_ref[...] = dot(current.astype(BF), pick_ref[tile_ref[0]], 1, 0).astype(BF)


def trace_steps_wide(got, far, owner, pick, traces, me, core):
    tiles, _, slots = got.shape
    half = slots // 2
    active = traces.shape[0] // 8
    frames = traces.shape[1]
    got, far = jnp.roll(got, tiles // 2, axis=0), jnp.roll(far, tiles // 2, axis=0)
    mine, theirs = got[:, :half].astype(F32), far[:, :half].astype(F32)
    gram = jnp.where(core == 0, jnp.concatenate([mine, theirs], axis=1), jnp.concatenate([theirs, mine], axis=1))
    drive = got[:, half : half + frames].astype(F32).transpose(0, 2, 1)
    tail = got[:, half + frames :].astype(F32)
    index = jax.vmap(lambda t: index_of(t, active))(tail).astype(jnp.int32).reshape(-1)
    bound = jnp.sum(tail[:, active : active + 3], axis=1).reshape(-1)
    bound = jax.ops.segment_sum(bound, index, num_segments=tiles * active)
    scale = (1.0 / (1.0 + bound))[:, None]
    current = tail[:, :active].reshape(tiles * active, frames)
    current = lax.dynamic_update_slice(current, traces[:active], (me * active, 0))

    def step(_, current):
        taken = jnp.take(current, index, axis=0).reshape(tiles, slots, frames)
        terms = jnp.einsum("tkj,tjf->tkf", gram, taken, precision=HIGHEST) - drive
        total = jax.ops.segment_sum(terms.reshape(-1, frames), index, num_segments=tiles * active)
        return jnp.maximum(current - total * scale, 0.0)

    current = lax.fori_loop(0, ITER_C, step, current)
    own = jnp.take(current, owner[0] * active + pick[0], axis=0)
    mine = lax.dynamic_slice(current, (me * active, 0), (active, frames))
    return mine.T, own.T.astype(BF)


def line_up_kernel(spot_ref, *refs):
    parts, out_ref = refs[:-1], refs[-1]
    for offset, part in enumerate(parts):
        out_ref[spot_ref[0] ^ offset] = part[...]


def sweep_kernel(spot_ref, tile_ref, foot_ref, traces_ref, cur_ref, rec_ref, *refs):
    lanes = rec_ref.shape[0]
    own_refs, refs = refs[:lanes], refs[lanes:]
    out_hbm, new_hbm, all_ref, own_ref, out_ref, new_ref, now_ref, add_ref, sems = refs
    owned = new_ref.shape[0]
    voxels, slots = foot_ref.shape
    active = owned // 8
    count = cur_ref.shape[1]
    all_ref[...] = cur_ref[...].T
    at = pl.multiple_of(tile_ref[0] * active if count > active else 0, 8)
    new_ref[:active, :] = all_ref[pl.ds(at, active), :]
    new_ref[active:, :] = jnp.maximum(traces_ref[active:, :], 0.0)
    copies = start(sems, [(new_ref, new_hbm)])
    for offset, part in enumerate(own_refs):
        own_ref[spot_ref[0] ^ offset] = part[...]
    own = jnp.concatenate([own_ref[lane] for lane in range(lanes)], axis=0)
    gram = dot(own, own, 0, 0)
    data = dot(jnp.concatenate([rec_ref[lane] for lane in range(lanes)], axis=1), own, 1, 0)
    step = 1.0 / (1.0 + jnp.sum(jnp.abs(gram), axis=0, keepdims=True))
    mix = jnp.concatenate(split(gram * step), axis=1)
    mix = jnp.concatenate([mix, mix], axis=0)
    foot = foot_ref[...].astype(F32)
    add_ref[...] = jnp.where(foot > 0, data * step, OFF)
    now_ref[...] = foot

    def swept(part):
        now = now_ref[part, :]
        moved = dot(jnp.concatenate(split(now), axis=1), mix, 1, 0)
        return jnp.maximum(now - (moved[:, :slots] + moved[:, slots:]) + add_ref[part, :], 0.0)

    for _ in range(ITER_A - 1):
        now_ref[...] = swept(slice(None))
    size = voxels // BLOCKS
    for block in range(BLOCKS):
        out_ref[block * size : (block + 1) * size, :] = swept(slice(block * size, (block + 1) * size)).astype(BF)
        part = pl.ds(block * size, size)
        copies += start(sems.at[pl.ds(1 + block, 1)], [(out_ref.at[part, :], out_hbm.at[part, :])])
    for copy in copies:
        copy.wait()


def body(recording, footprints, slot_owner, slot_pick, traces):
    tiles = lax.axis_size("tile")
    lanes = lax.axis_size("frame")
    voxels, slots = footprints.shape
    owned, frames = traces.shape
    active = owned // 8
    half = slots // 2
    count = tiles * active
    me = lax.axis_index("tile").astype(jnp.int32)[None]
    spot = lax.axis_index("frame").astype(jnp.int32)[None]
    core = spot & 1
    owner = slot_owner.reshape(1, slots)
    pick = slot_pick.reshape(1, slots)
    rows = half + frames + active + META

    def swap(value, bit):
        return lax.ppermute(value, "frame", [(i, i ^ bit) for i in range(lanes)])

    def shape(dims, dtype=F32):
        return jax.ShapeDtypeStruct(dims, dtype)

    packed = pl.pallas_call(
        pack_kernel,
        out_shape=shape((tiles, rows, slots), BF),
        in_specs=[SMEM] + [HBM] * 5,
        out_specs=VMEM,
        scratch_shapes=[
            pltpu.VMEM((voxels, slots), BF),
            pltpu.VMEM((voxels, frames), BF),
            pltpu.VMEM((1, slots), jnp.int32),
            pltpu.VMEM((1, slots), jnp.int32),
            pltpu.VMEM((active, frames), F32),
            pltpu.VMEM((slots, slots), BF),
            pltpu.SemaphoreType.DMA((5,)),
        ],
        name="pack",
    )(core, footprints, recording, owner, pick, traces)
    order = [(tile + tiles // 2) % tiles for tile in range(tiles)]
    got = lax.all_to_all(packed, "tile", split_axis=0, concat_axis=0, axis_index_groups=[order], tiled=True)

    blocks = [recording] + [swap(recording, bit) for bit in range(2, lanes, 2)]
    blocks = [part for block in blocks for part in (block, swap(block, 1))]
    lined = pl.pallas_call(
        line_up_kernel,
        out_shape=shape((lanes, voxels, frames), BF),
        in_specs=[SMEM] + [VMEM] * lanes,
        out_specs=VMEM,
        compiler_params=PARAMS,
        name="line_up",
    )(spot, *blocks)
    got, lined = lax.optimization_barrier((got, lined))
    far = swap(got, 1)
    if count <= DENSE_LIMIT:
        begun = pl.pallas_call(
            begin_kernel,
            out_shape=(
                shape((tiles, count, slots), BF),
                shape((frames, count)),
                shape((8, count)),
                shape((frames, count)),
            ),
            in_specs=[SMEM, VMEM, HBM],
            out_specs=(VMEM,) * 4,
            scratch_shapes=[pltpu.VMEM((count, frames), F32), pltpu.SemaphoreType.DMA((1,))],
            compiler_params=PARAMS,
            name="begin",
        )(me, got, traces)
        current, own = pl.pallas_call(
            trace_kernel,
            out_shape=(shape((frames, count)), shape((frames, slots), BF)),
            in_specs=[SMEM] * 2 + [VMEM] * 6,
            out_specs=(VMEM,) * 2,
            scratch_shapes=[pltpu.VMEM((tiles, slots, slots), BF)],
            compiler_params=PARAMS,
            name="traces",
        )(core, me, got, far, *begun)
    else:
        current, own = trace_steps_wide(got, far, owner, pick, traces, me[0], core[0])
    every = [own] + [swap(own, bit) for bit in range(1, lanes)]
    updated, new_traces = pl.pallas_call(
        sweep_kernel,
        out_shape=(shape((voxels, slots), BF), shape((owned, frames))),
        in_specs=[SMEM] * 2 + [VMEM] * (4 + lanes),
        out_specs=(HBM, HBM),
        scratch_shapes=[
            pltpu.VMEM(current.shape[::-1], F32),
            pltpu.VMEM((lanes, frames, slots), BF),
            pltpu.VMEM((voxels, slots), BF),
            pltpu.VMEM((owned, frames), F32),
            pltpu.VMEM((voxels, slots), F32),
            pltpu.VMEM((voxels, slots), F32),
            pltpu.SemaphoreType.DMA((1 + BLOCKS,)),
        ],
        compiler_params=PARAMS,
        name="sweeps",
    )(spot, me, footprints, traces, current, lined, *every)
    return (new_traces, updated)


def solution(mesh):
    in_specs = (P("tile", "frame"), P("tile", None), P("tile", None), P("tile"), P("tile", "frame"))
    out_specs = (P("tile", "frame"), P("tile", None))
    return jax.shard_map(body, mesh=mesh, in_specs=in_specs, out_specs=out_specs, check_vma=False)
```

```python
import jax
import jax.numpy as jnp
from jax import lax
from jax.experimental import pallas as pl
from jax.experimental.pallas import tpu as pltpu
from jax.sharding import PartitionSpec as P

ITER_C = 4
ITER_A = 8
META = 8
BLOCKS = 4
DENSE_LIMIT = 1024
OFF = -1e30
BF = jnp.bfloat16
F32 = jnp.float32
VMEM = pl.BlockSpec(memory_space=pltpu.VMEM)
SMEM = pl.BlockSpec(memory_space=pltpu.SMEM)
HBM = pl.BlockSpec(memory_space=pltpu.MemorySpace.HBM)
HIGHEST = lax.Precision.HIGHEST
PARAMS = pltpu.CompilerParams(vmem_limit_bytes=16 << 20)


def dot(a, b, ca, cb, precision=None):
    return lax.dot_general(a, b, (((ca,), (cb,)), ((), ())), precision=precision, preferred_element_type=F32)


def split(x):
    high = x.astype(BF)
    return high, (x - high.astype(F32)).astype(BF)


def place(source, tiles):
    return (source - tiles // 2) % tiles


def start(sems, pairs):
    copies = [pltpu.make_async_copy(source, target, sems.at[i]) for i, (source, target) in enumerate(pairs)]
    for copy in copies:
        copy.start()
    return copies


def pack_kernel(core_ref, foot_hbm, rec_hbm, owner_hbm, pick_hbm, traces_hbm, out_ref, foot_ref, rec_ref, owner_ref, pick_ref, traces_ref, gram_ref, sems):
    tiles = out_ref.shape[0]
    slots = foot_ref.shape[1]
    frames = rec_ref.shape[1]
    half = slots // 2
    active = traces_ref.shape[0]
    copies = start(
        sems,
        [
            (foot_hbm, foot_ref),
            (rec_hbm, rec_ref),
            (owner_hbm, owner_ref),
            (pick_hbm, pick_ref),
            (traces_hbm.at[pl.ds(0, active), :], traces_ref),
        ],
    )
    for copy in copies:
        copy.wait()
    foot = foot_ref[...]
    both = dot(foot, jnp.concatenate([foot, rec_ref[...]], axis=1), 0, 0)
    gram, drive = both[:, :slots], both[:, slots:].T.astype(BF)
    bound = jnp.sum(jnp.abs(gram), axis=0, keepdims=True)
    high = bound.astype(BF).astype(F32)
    middle = (bound - high).astype(BF).astype(F32)
    low = bound - high - middle
    named = [high, middle, low, owner_ref[...].astype(F32), pick_ref[...].astype(F32)]
    rest = jnp.zeros((META - len(named), slots), F32)
    tail = jnp.concatenate([traces_ref[...]] + named + [rest], axis=0).astype(BF)
    gram_ref[...] = gram.astype(BF)
    gram = gram_ref[pl.ds(pl.multiple_of(core_ref[0] * half, 16), half), :]
    for tile in range(tiles):
        out_ref[tile, 0:half, :] = gram
        out_ref[tile, half : half + frames, :] = drive
        out_ref[tile, half + frames : half + frames + active + META, :] = tail


def index_of(tail, active):
    meta = tail[active : active + META]
    return meta[3:4] * float(active) + meta[4:5]


def begin_kernel(tile_ref, got_ref, traces_hbm, pick_ref, pull_ref, scale_ref, cur_ref, first_ref, sems):
    tiles, rows, slots = got_ref.shape
    frames = cur_ref.shape[0]
    half = slots // 2
    active = rows - half - frames - META
    count = tiles * active
    row = lax.broadcasted_iota(jnp.int32, (count, slots), 0).astype(F32)
    for tile in range(tiles):
        tail = got_ref[place(tile, tiles), half + frames :, :].astype(F32)
        first_ref[tile * active : (tile + 1) * active, :] = tail[:active]
        pick_ref[tile] = jnp.where(row == index_of(tail, active), 1.0, 0.0).astype(BF)
    at = pl.multiple_of(tile_ref[0] * active, 8)
    copies = start(sems, [(traces_hbm.at[pl.ds(0, active), :], first_ref.at[pl.ds(at, active), :])])
    pick = jnp.concatenate([pick_ref[tile] for tile in range(tiles)], axis=1)
    parts = jnp.concatenate([got_ref[place(tile, tiles), half:, :] for tile in range(tiles)], axis=1)
    sums = dot(parts, pick, 1, 1)
    pull_ref[...] = sums[:frames]
    bound = sums[frames + active : frames + active + META]
    scale_ref[...] = jnp.broadcast_to(1.0 / (1.0 + bound[0:1] + bound[1:2] + bound[2:3]), scale_ref.shape)
    for copy in copies:
        copy.wait()
    cur_ref[...] = first_ref[...].T


def trace_kernel(core_ref, tile_ref, got_ref, far_ref, pick_ref, pull_ref, scale_ref, cur_ref, new_ref, own_ref, gram_ref):
    tiles, count, slots = pick_ref.shape
    half = slots // 2
    here = pl.multiple_of(core_ref[0] * half, 16)
    there = pl.multiple_of((1 - core_ref[0]) * half, 16)
    mixed = []
    for tile in range(tiles):
        gram_ref[tile, pl.ds(here, half), :] = got_ref[place(tile, tiles), :half, :]
        gram_ref[tile, pl.ds(there, half), :] = far_ref[place(tile, tiles), :half, :]
        mixed.append(dot(pick_ref[tile], gram_ref[tile], 1, 0).astype(BF))
    pick = jnp.concatenate([pick_ref[tile] for tile in range(tiles)], axis=1)
    whole = dot(jnp.concatenate(mixed, axis=1), pick, 1, 1).astype(BF)
    pull, scale, current = pull_ref[...], scale_ref[0:1, :], cur_ref[...]
    for _ in range(ITER_C):
        push = dot(current.astype(BF), whole, 1, 0)
        current = jnp.maximum(current - (push - pull) * scale, 0.0)
    new_ref[...] = current
    own_ref[...] = dot(current.astype(BF), pick_ref[tile_ref[0]], 1, 0).astype(BF)


def trace_steps_wide(got, far, owner, pick, traces, me, core):
    tiles, _, slots = got.shape
    half = slots // 2
    active = traces.shape[0] // 8
    frames = traces.shape[1]
    got, far = jnp.roll(got, tiles // 2, axis=0), jnp.roll(far, tiles // 2, axis=0)
    mine, theirs = got[:, :half].astype(F32), far[:, :half].astype(F32)
    gram = jnp.where(core == 0, jnp.concatenate([mine, theirs], axis=1), jnp.concatenate([theirs, mine], axis=1))
    drive = got[:, half : half + frames].astype(F32).transpose(0, 2, 1)
    tail = got[:, half + frames :].astype(F32)
    index = jax.vmap(lambda t: index_of(t, active))(tail).astype(jnp.int32).reshape(-1)
    bound = jnp.sum(tail[:, active : active + 3], axis=1).reshape(-1)
    bound = jax.ops.segment_sum(bound, index, num_segments=tiles * active)
    scale = (1.0 / (1.0 + bound))[:, None]
    current = tail[:, :active].reshape(tiles * active, frames)
    current = lax.dynamic_update_slice(current, traces[:active], (me * active, 0))

    def step(_, current):
        taken = jnp.take(current, index, axis=0).reshape(tiles, slots, frames)
        terms = jnp.einsum("tkj,tjf->tkf", gram, taken, precision=HIGHEST) - drive
        total = jax.ops.segment_sum(terms.reshape(-1, frames), index, num_segments=tiles * active)
        return jnp.maximum(current - total * scale, 0.0)

    current = lax.fori_loop(0, ITER_C, step, current)
    own = jnp.take(current, owner[0] * active + pick[0], axis=0)
    mine = lax.dynamic_slice(current, (me * active, 0), (active, frames))
    return mine.T, own.T.astype(BF)


def line_up_kernel(spot_ref, *refs):
    parts, out_ref = refs[:-1], refs[-1]
    for offset, part in enumerate(parts):
        out_ref[spot_ref[0] ^ offset] = part[...]


def pair_sums(lane, rec_ref, own_refs, own_ref):
    for bit, part in enumerate(own_refs):
        own_ref[(lane ^ bit) & 1] = part[...]
    own = jnp.concatenate([own_ref[0], own_ref[1]], axis=0)
    first = lane & -2
    rec = jnp.concatenate([rec_ref[first], rec_ref[first + 1]], axis=1)
    return dot(own, own, 0, 0), dot(rec, own, 1, 0)


def early_kernel(spot_ref, tile_ref, traces_ref, cur_ref, rec_ref, own_ref, near_ref, new_hbm, gram_ref, data_ref, all_ref, pair_ref, new_ref, sems):
    owned = new_ref.shape[0]
    active = owned // 8
    all_ref[...] = cur_ref[...].T
    at = pl.multiple_of(tile_ref[0] * active if cur_ref.shape[1] > active else 0, 8)
    new_ref[:active, :] = all_ref[pl.ds(at, active), :]
    new_ref[active:, :] = jnp.maximum(traces_ref[active:, :], 0.0)
    copies = start(sems, [(new_ref, new_hbm)])
    gram_ref[...], data_ref[...] = pair_sums(spot_ref[0], rec_ref, (own_ref, near_ref), pair_ref)
    for copy in copies:
        copy.wait()


def sweep_kernel(spot_ref, foot_ref, rec_ref, gram_ref, data_ref, *refs):
    lanes = rec_ref.shape[0]
    own_refs, refs = refs[: lanes - 2], refs[lanes - 2 :]
    out_hbm, pair_ref, out_ref, now_ref, add_ref, sems = refs
    voxels, slots = foot_ref.shape
    gram, data = gram_ref[...], data_ref[...]
    for offset in range(2, lanes, 2):
        more, extra = pair_sums(spot_ref[0] ^ offset, rec_ref, own_refs[offset - 2 : offset], pair_ref)
        gram, data = gram + more, data + extra
    step = 1.0 / (1.0 + jnp.sum(jnp.abs(gram), axis=0, keepdims=True))
    mix = jnp.concatenate(split(gram * step), axis=1)
    foot = foot_ref[...].astype(F32)
    add_ref[...] = jnp.where(foot > 0, data * step, OFF)
    now_ref[...] = foot

    def swept(part):
        now = now_ref[part, :]
        moved = dot(now.astype(BF), mix, 1, 0)
        return jnp.maximum(now - (moved[:, :slots] + moved[:, slots:]) + add_ref[part, :], 0.0)

    for _ in range(ITER_A - 1):
        now_ref[...] = swept(slice(None))
    size = voxels // BLOCKS
    copies = []
    for block in range(BLOCKS):
        out_ref[block * size : (block + 1) * size, :] = swept(slice(block * size, (block + 1) * size)).astype(BF)
        part = pl.ds(block * size, size)
        copies += start(sems.at[pl.ds(block, 1)], [(out_ref.at[part, :], out_hbm.at[part, :])])
    for copy in copies:
        copy.wait()


def body(recording, footprints, slot_owner, slot_pick, traces):
    tiles = lax.axis_size("tile")
    lanes = lax.axis_size("frame")
    voxels, slots = footprints.shape
    owned, frames = traces.shape
    active = owned // 8
    half = slots // 2
    count = tiles * active
    me = lax.axis_index("tile").astype(jnp.int32)[None]
    spot = lax.axis_index("frame").astype(jnp.int32)[None]
    core = spot & 1
    owner = slot_owner.reshape(1, slots)
    pick = slot_pick.reshape(1, slots)
    rows = half + frames + active + META

    def swap(value, bit):
        return lax.ppermute(value, "frame", [(i, i ^ bit) for i in range(lanes)])

    def shape(dims, dtype=F32):
        return jax.ShapeDtypeStruct(dims, dtype)

    packed = pl.pallas_call(
        pack_kernel,
        out_shape=shape((tiles, rows, slots), BF),
        in_specs=[SMEM] + [HBM] * 5,
        out_specs=VMEM,
        scratch_shapes=[
            pltpu.VMEM((voxels, slots), BF),
            pltpu.VMEM((voxels, frames), BF),
            pltpu.VMEM((1, slots), jnp.int32),
            pltpu.VMEM((1, slots), jnp.int32),
            pltpu.VMEM((active, frames), F32),
            pltpu.VMEM((slots, slots), BF),
            pltpu.SemaphoreType.DMA((5,)),
        ],
        name="pack",
    )(core, footprints, recording, owner, pick, traces)
    order = [(tile + tiles // 2) % tiles for tile in range(tiles)]
    got = lax.all_to_all(packed, "tile", split_axis=0, concat_axis=0, axis_index_groups=[order], tiled=True)

    blocks = [recording] + [swap(recording, bit) for bit in range(2, lanes, 2)]
    blocks = [part for block in blocks for part in (block, swap(block, 1))]
    lined = pl.pallas_call(
        line_up_kernel,
        out_shape=shape((lanes, voxels, frames), BF),
        in_specs=[SMEM] + [VMEM] * lanes,
        out_specs=VMEM,
        compiler_params=PARAMS,
        name="line_up",
    )(spot, *blocks)
    got, lined = lax.optimization_barrier((got, lined))
    far = swap(got, 1)
    if count <= DENSE_LIMIT:
        begun = pl.pallas_call(
            begin_kernel,
            out_shape=(
                shape((tiles, count, slots), BF),
                shape((frames, count)),
                shape((8, count)),
                shape((frames, count)),
            ),
            in_specs=[SMEM, VMEM, HBM],
            out_specs=(VMEM,) * 4,
            scratch_shapes=[pltpu.VMEM((count, frames), F32), pltpu.SemaphoreType.DMA((1,))],
            compiler_params=PARAMS,
            name="begin",
        )(me, got, traces)
        current, own = pl.pallas_call(
            trace_kernel,
            out_shape=(shape((frames, count)), shape((frames, slots), BF)),
            in_specs=[SMEM] * 2 + [VMEM] * 6,
            out_specs=(VMEM,) * 2,
            scratch_shapes=[pltpu.VMEM((tiles, slots, slots), BF)],
            compiler_params=PARAMS,
            name="traces",
        )(core, me, got, far, *begun)
    else:
        current, own = trace_steps_wide(got, far, owner, pick, traces, me[0], core[0])
    others = [swap(own, bit) for bit in range(1, lanes)]
    new_traces, gram, data = pl.pallas_call(
        early_kernel,
        out_shape=(shape((owned, frames)), shape((slots, slots)), shape((voxels, slots))),
        in_specs=[SMEM] * 2 + [VMEM] * 5,
        out_specs=(HBM, VMEM, VMEM),
        scratch_shapes=[
            pltpu.VMEM(current.shape[::-1], F32),
            pltpu.VMEM((2, frames, slots), BF),
            pltpu.VMEM((owned, frames), F32),
            pltpu.SemaphoreType.DMA((1,)),
        ],
        compiler_params=PARAMS,
        name="early",
    )(spot, me, traces, current, lined, own, others[0])
    updated = pl.pallas_call(
        sweep_kernel,
        out_shape=shape((voxels, slots), BF),
        in_specs=[SMEM] + [VMEM] * (4 + len(others) - 1),
        out_specs=HBM,
        scratch_shapes=[
            pltpu.VMEM((2, frames, slots), BF),
            pltpu.VMEM((voxels, slots), BF),
            pltpu.VMEM((voxels, slots), F32),
            pltpu.VMEM((voxels, slots), F32),
            pltpu.SemaphoreType.DMA((BLOCKS,)),
        ],
        compiler_params=PARAMS,
        name="sweeps",
    )(spot, footprints, lined, gram, data, *others[1:])
    return (new_traces, updated)


def solution(mesh):
    in_specs = (P("tile", "frame"), P("tile", None), P("tile", None), P("tile"), P("tile", "frame"))
    out_specs = (P("tile", "frame"), P("tile", None))
    return jax.shard_map(body, mesh=mesh, in_specs=in_specs, out_specs=out_specs, check_vma=False)
```

```python
import jax
import jax.numpy as jnp
from jax import lax
from jax.experimental import pallas as pl
from jax.experimental.pallas import tpu as pltpu
from jax.sharding import PartitionSpec as P

ITER_C = 4
ITER_A = 8
META = 8
BLOCKS = 4
DENSE_LIMIT = 1024
OFF = -1e30
BF = jnp.bfloat16
F32 = jnp.float32
VMEM = pl.BlockSpec(memory_space=pltpu.VMEM)
SMEM = pl.BlockSpec(memory_space=pltpu.SMEM)
HBM = pl.BlockSpec(memory_space=pltpu.MemorySpace.HBM)
HIGHEST = lax.Precision.HIGHEST
PARAMS = pltpu.CompilerParams(vmem_limit_bytes=16 << 20)


def dot(a, b, ca, cb, precision=None):
    return lax.dot_general(a, b, (((ca,), (cb,)), ((), ())), precision=precision, preferred_element_type=F32)


def split(x):
    high = x.astype(BF)
    return high, (x - high.astype(F32)).astype(BF)


def place(source, tiles):
    return (source - tiles // 2) % tiles


def start(sems, pairs):
    copies = [pltpu.make_async_copy(source, target, sems.at[i]) for i, (source, target) in enumerate(pairs)]
    for copy in copies:
        copy.start()
    return copies


def pack_kernel(core_ref, foot_hbm, rec_hbm, owner_hbm, pick_hbm, traces_hbm, out_ref, foot_ref, rec_ref, owner_ref, pick_ref, traces_ref, gram_ref, sems):
    tiles = out_ref.shape[0]
    slots = foot_ref.shape[1]
    frames = rec_ref.shape[1]
    half = slots // 2
    active = traces_ref.shape[0]
    copies = start(
        sems,
        [
            (foot_hbm, foot_ref),
            (rec_hbm, rec_ref),
            (owner_hbm, owner_ref),
            (pick_hbm, pick_ref),
            (traces_hbm.at[pl.ds(0, active), :], traces_ref),
        ],
    )
    for copy in copies:
        copy.wait()
    foot = foot_ref[...]
    both = dot(foot, jnp.concatenate([foot, rec_ref[...]], axis=1), 0, 0)
    gram, drive = both[:, :slots], both[:, slots:].T.astype(BF)
    bound = jnp.sum(jnp.abs(gram), axis=0, keepdims=True)
    high = bound.astype(BF).astype(F32)
    middle = (bound - high).astype(BF).astype(F32)
    low = bound - high - middle
    named = [high, middle, low, owner_ref[...].astype(F32), pick_ref[...].astype(F32)]
    rest = jnp.zeros((META - len(named), slots), F32)
    tail = jnp.concatenate([traces_ref[...]] + named + [rest], axis=0).astype(BF)
    gram_ref[...] = gram.astype(BF)
    gram = gram_ref[pl.ds(pl.multiple_of(core_ref[0] * half, 16), half), :]
    for tile in range(tiles):
        out_ref[tile, 0:half, :] = gram
        out_ref[tile, half : half + frames, :] = drive
        out_ref[tile, half + frames : half + frames + active + META, :] = tail


def index_of(tail, active):
    meta = tail[active : active + META]
    return meta[3:4] * float(active) + meta[4:5]


def begin_kernel(tile_ref, got_ref, traces_hbm, pick_ref, pull_ref, scale_ref, cur_ref, first_ref, sems):
    tiles, rows, slots = got_ref.shape
    frames = cur_ref.shape[0]
    half = slots // 2
    active = rows - half - frames - META
    count = tiles * active
    row = lax.broadcasted_iota(jnp.int32, (count, slots), 0).astype(F32)
    for tile in range(tiles):
        tail = got_ref[place(tile, tiles), half + frames :, :].astype(F32)
        first_ref[tile * active : (tile + 1) * active, :] = tail[:active]
        pick_ref[tile] = jnp.where(row == index_of(tail, active), 1.0, 0.0).astype(BF)
    at = pl.multiple_of(tile_ref[0] * active, 8)
    copies = start(sems, [(traces_hbm.at[pl.ds(0, active), :], first_ref.at[pl.ds(at, active), :])])
    pick = jnp.concatenate([pick_ref[tile] for tile in range(tiles)], axis=1)
    parts = jnp.concatenate([got_ref[place(tile, tiles), half:, :] for tile in range(tiles)], axis=1)
    sums = dot(parts, pick, 1, 1)
    pull_ref[...] = sums[:frames]
    bound = sums[frames + active : frames + active + META]
    scale_ref[...] = jnp.broadcast_to(1.0 / (1.0 + bound[0:1] + bound[1:2] + bound[2:3]), scale_ref.shape)
    for copy in copies:
        copy.wait()
    cur_ref[...] = first_ref[...].T


def trace_kernel(core_ref, tile_ref, got_ref, far_ref, near_ref, pick_ref, pull_ref, scale_ref, cur_ref, new_ref, own_ref, gram_ref, first_ref, both_ref, drawn_ref):
    tiles, count, slots = pick_ref.shape
    half = slots // 2
    frames = cur_ref.shape[0]
    active = count // tiles
    core = core_ref[0]
    here = pl.multiple_of(core * half, 16)
    there = pl.multiple_of((1 - core) * half, 16)
    mixed, parts = [], []
    for tile in range(tiles):
        spot = place(tile, tiles)
        gram_ref[tile, pl.ds(here, half), :] = got_ref[spot, :half, :]
        gram_ref[tile, pl.ds(there, half), :] = far_ref[spot, :half, :]
        first_ref[tile * active : (tile + 1) * active, :] = far_ref[spot, half + frames :, :].astype(F32)[:active]
        parts.append(far_ref[spot, half : half + frames, :])
        mixed.append(dot(pick_ref[tile], gram_ref[tile], 1, 0).astype(BF))
    first_ref[pl.ds(pl.multiple_of(tile_ref[0] * active, 8), active), :] = near_ref[...]
    pick = jnp.concatenate([pick_ref[tile] for tile in range(tiles)], axis=1)
    whole = dot(jnp.concatenate(mixed, axis=1), pick, 1, 1).astype(BF)
    both_ref[core] = cur_ref[...]
    both_ref[1 - core] = first_ref[...].T
    drawn_ref[core] = pull_ref[...]
    drawn_ref[1 - core] = dot(jnp.concatenate(parts, axis=1), pick, 1, 1)
    pull = jnp.concatenate([drawn_ref[0], drawn_ref[1]], axis=0)
    current = jnp.concatenate([both_ref[0], both_ref[1]], axis=0)
    scale = scale_ref[0:1, :]
    for _ in range(ITER_C):
        push = dot(current.astype(BF), whole, 1, 0)
        current = jnp.maximum(current - (push - pull) * scale, 0.0)
    own_ref[...] = dot(current.astype(BF), pick_ref[tile_ref[0]], 1, 0).astype(BF)
    both_ref[0], both_ref[1] = current[:frames], current[frames:]
    new_ref[...] = both_ref[core]


def trace_steps_wide(got, far, near, owner, pick, traces, me, core):
    tiles, _, slots = got.shape
    half = slots // 2
    active = traces.shape[0] // 8
    frames = traces.shape[1]
    count = tiles * active
    got, far = jnp.roll(got, tiles // 2, axis=0), jnp.roll(far, tiles // 2, axis=0)
    tail = got[:, half + frames :].astype(F32)
    index = jax.vmap(lambda t: index_of(t, active))(tail).astype(jnp.int32).reshape(tiles, slots)
    bound = jnp.sum(tail[:, active : active + 3], axis=1).reshape(-1)
    bound = jax.ops.segment_sum(bound, index.reshape(-1), num_segments=count)
    scale = (1.0 / (1.0 + bound))[:, None]

    def in_order(ours, others, axis):
        return jnp.where(core == 0, jnp.concatenate([ours, others], axis=axis), jnp.concatenate([others, ours], axis=axis))

    def rows_of(block, exact):
        rows = block[:, half + frames : half + frames + active].astype(F32).reshape(count, frames)
        return lax.dynamic_update_slice(rows, exact, (me * active, 0))

    def step(_, current):
        def add(total, parts):
            ours, others, rows = parts
            gram = in_order(ours[:half], others[:half], 0).astype(F32)
            drive = in_order(ours[half : half + frames], others[half : half + frames], 0).astype(F32).T
            terms = dot(gram, jnp.take(current, rows, axis=0), 1, 0, HIGHEST) - drive
            return total.at[rows].add(terms), None

        total, _ = lax.scan(add, jnp.zeros_like(current), (got, far, index))
        return jnp.maximum(current - total * scale, 0.0)

    current = lax.fori_loop(0, ITER_C, step, in_order(rows_of(got, traces[:active]), rows_of(far, near), 1))
    own = jnp.take(current, owner[0] * active + pick[0], axis=0)
    mine = lax.dynamic_slice(current, (me * active, core * frames), (active, frames))
    return mine.T, own.T.astype(BF)


def line_up_kernel(spot_ref, *refs):
    parts, out_ref = refs[:-1], refs[-1]
    for offset, part in enumerate(parts):
        out_ref[spot_ref[0] ^ offset] = part[...]


def pair_sums(lane, rec_ref, own):
    first = lane & -2
    rec = jnp.concatenate([rec_ref[first], rec_ref[first + 1]], axis=1)
    return dot(own, own, 0, 0), dot(rec, own, 1, 0)


def early_kernel(spot_ref, tile_ref, traces_ref, cur_ref, rec_ref, own_ref, new_hbm, gram_ref, data_ref, all_ref, new_ref, sems):
    owned = new_ref.shape[0]
    active = owned // 8
    all_ref[...] = cur_ref[...].T
    at = pl.multiple_of(tile_ref[0] * active if cur_ref.shape[1] > active else 0, 8)
    new_ref[:active, :] = all_ref[pl.ds(at, active), :]
    new_ref[active:, :] = jnp.maximum(traces_ref[active:, :], 0.0)
    copies = start(sems, [(new_ref, new_hbm)])
    gram_ref[...], data_ref[...] = pair_sums(spot_ref[0], rec_ref, own_ref[...])
    for copy in copies:
        copy.wait()


def sweep_kernel(spot_ref, foot_ref, rec_ref, gram_ref, data_ref, *refs):
    lanes = rec_ref.shape[0]
    own_refs, refs = refs[: lanes // 2 - 1], refs[lanes // 2 - 1 :]
    out_hbm, out_ref, now_ref, add_ref, sems = refs
    voxels, slots = foot_ref.shape
    gram, data = gram_ref[...], data_ref[...]
    for offset, own_ref in zip(range(2, lanes, 2), own_refs):
        more, extra = pair_sums(spot_ref[0] ^ offset, rec_ref, own_ref[...])
        gram, data = gram + more, data + extra
    step = 1.0 / (1.0 + jnp.sum(jnp.abs(gram), axis=0, keepdims=True))
    mix = jnp.concatenate(split(gram * step), axis=1)
    foot = foot_ref[...].astype(F32)
    add_ref[...] = jnp.where(foot > 0, data * step, OFF)
    now_ref[...] = foot

    def swept(part):
        now = now_ref[part, :]
        moved = dot(now.astype(BF), mix, 1, 0)
        return jnp.maximum(now - (moved[:, :slots] + moved[:, slots:]) + add_ref[part, :], 0.0)

    for _ in range(ITER_A - 1):
        now_ref[...] = swept(slice(None))
    size = voxels // BLOCKS
    copies = []
    for block in range(BLOCKS):
        out_ref[block * size : (block + 1) * size, :] = swept(slice(block * size, (block + 1) * size)).astype(BF)
        part = pl.ds(block * size, size)
        copies += start(sems.at[pl.ds(block, 1)], [(out_ref.at[part, :], out_hbm.at[part, :])])
    for copy in copies:
        copy.wait()


def body(recording, footprints, slot_owner, slot_pick, traces):
    tiles = lax.axis_size("tile")
    lanes = lax.axis_size("frame")
    voxels, slots = footprints.shape
    owned, frames = traces.shape
    active = owned // 8
    half = slots // 2
    count = tiles * active
    me = lax.axis_index("tile").astype(jnp.int32)[None]
    spot = lax.axis_index("frame").astype(jnp.int32)[None]
    core = spot & 1
    owner = slot_owner.reshape(1, slots)
    pick = slot_pick.reshape(1, slots)
    rows = half + frames + active + META

    def swap(value, bit):
        return lax.ppermute(value, "frame", [(i, i ^ bit) for i in range(lanes)])

    def shape(dims, dtype=F32):
        return jax.ShapeDtypeStruct(dims, dtype)

    packed = pl.pallas_call(
        pack_kernel,
        out_shape=shape((tiles, rows, slots), BF),
        in_specs=[SMEM] + [HBM] * 5,
        out_specs=VMEM,
        scratch_shapes=[
            pltpu.VMEM((voxels, slots), BF),
            pltpu.VMEM((voxels, frames), BF),
            pltpu.VMEM((1, slots), jnp.int32),
            pltpu.VMEM((1, slots), jnp.int32),
            pltpu.VMEM((active, frames), F32),
            pltpu.VMEM((slots, slots), BF),
            pltpu.SemaphoreType.DMA((5,)),
        ],
        name="pack",
    )(core, footprints, recording, owner, pick, traces)
    order = [(tile + tiles // 2) % tiles for tile in range(tiles)]
    got = lax.all_to_all(packed, "tile", split_axis=0, concat_axis=0, axis_index_groups=[order], tiled=True)

    blocks = [recording] + [swap(recording, bit) for bit in range(2, lanes, 2)]
    blocks = [part for block in blocks for part in (block, swap(block, 1))]
    lined = pl.pallas_call(
        line_up_kernel,
        out_shape=shape((lanes, voxels, frames), BF),
        in_specs=[SMEM] + [VMEM] * lanes,
        out_specs=VMEM,
        compiler_params=PARAMS,
        name="line_up",
    )(spot, *blocks)
    near = swap(traces[:active], 1)
    got, lined, near = lax.optimization_barrier((got, lined, near))
    far = swap(got, 1)
    if count <= DENSE_LIMIT:
        begun = pl.pallas_call(
            begin_kernel,
            out_shape=(
                shape((tiles, count, slots), BF),
                shape((frames, count)),
                shape((8, count)),
                shape((frames, count)),
            ),
            in_specs=[SMEM, VMEM, HBM],
            out_specs=(VMEM,) * 4,
            scratch_shapes=[pltpu.VMEM((count, frames), F32), pltpu.SemaphoreType.DMA((1,))],
            compiler_params=PARAMS,
            name="begin",
        )(me, got, traces)
        current, own = pl.pallas_call(
            trace_kernel,
            out_shape=(shape((frames, count)), shape((2 * frames, slots), BF)),
            in_specs=[SMEM] * 2 + [VMEM] * 7,
            out_specs=(VMEM,) * 2,
            scratch_shapes=[
                pltpu.VMEM((tiles, slots, slots), BF),
                pltpu.VMEM((count, frames), F32),
                pltpu.VMEM((2, frames, count), F32),
                pltpu.VMEM((2, frames, count), F32),
            ],
            compiler_params=PARAMS,
            name="traces",
        )(core, me, got, far, near, *begun)
    else:
        current, own = trace_steps_wide(got, far, near, owner, pick, traces, me[0], core[0])
    others = [swap(own, bit) for bit in range(2, lanes, 2)]
    new_traces, gram, data = pl.pallas_call(
        early_kernel,
        out_shape=(shape((owned, frames)), shape((slots, slots)), shape((voxels, slots))),
        in_specs=[SMEM] * 2 + [VMEM] * 4,
        out_specs=(HBM, VMEM, VMEM),
        scratch_shapes=[
            pltpu.VMEM(current.shape[::-1], F32),
            pltpu.VMEM((owned, frames), F32),
            pltpu.SemaphoreType.DMA((1,)),
        ],
        compiler_params=PARAMS,
        name="early",
    )(spot, me, traces, current, lined, own)
    updated = pl.pallas_call(
        sweep_kernel,
        out_shape=shape((voxels, slots), BF),
        in_specs=[SMEM] + [VMEM] * (4 + len(others)),
        out_specs=HBM,
        scratch_shapes=[
            pltpu.VMEM((voxels, slots), BF),
            pltpu.VMEM((voxels, slots), F32),
            pltpu.VMEM((voxels, slots), F32),
            pltpu.SemaphoreType.DMA((BLOCKS,)),
        ],
        compiler_params=PARAMS,
        name="sweeps",
    )(spot, footprints, lined, gram, data, *others)
    return (new_traces, updated)


def solution(mesh):
    in_specs = (P("tile", "frame"), P("tile", None), P("tile", None), P("tile"), P("tile", "frame"))
    out_specs = (P("tile", "frame"), P("tile", None))
    return jax.shard_map(body, mesh=mesh, in_specs=in_specs, out_specs=out_specs, check_vma=False)
```

```python
import jax
import jax.numpy as jnp
from jax import lax
from jax.experimental import pallas as pl
from jax.experimental.pallas import tpu as pltpu
from jax.sharding import PartitionSpec as P

ITER_C = 4
ITER_A = 8
META = 8
BLOCKS = 4
DENSE_LIMIT = 1024
OFF = -1e30
BF = jnp.bfloat16
F32 = jnp.float32
VMEM = pl.BlockSpec(memory_space=pltpu.VMEM)
SMEM = pl.BlockSpec(memory_space=pltpu.SMEM)
HBM = pl.BlockSpec(memory_space=pltpu.MemorySpace.HBM)
HIGHEST = lax.Precision.HIGHEST
PARAMS = pltpu.CompilerParams(vmem_limit_bytes=16 << 20)


def dot(a, b, ca, cb, precision=None):
    return lax.dot_general(a, b, (((ca,), (cb,)), ((), ())), precision=precision, preferred_element_type=F32)


def split(x):
    high = x.astype(BF)
    return high, (x - high.astype(F32)).astype(BF)


def order_of(tiles):
    return sorted(range(tiles), key=lambda tile: (tile % 2, (tiles // 2 - tile + tile % 2) % tiles))


def place(source, tiles):
    return order_of(tiles).index(source)


def start(sems, pairs):
    copies = [pltpu.make_async_copy(source, target, sems.at[i]) for i, (source, target) in enumerate(pairs)]
    for copy in copies:
        copy.start()
    return copies


def pack_kernel(core_ref, foot_hbm, rec_hbm, owner_hbm, pick_hbm, traces_hbm, out_ref, foot_ref, rec_ref, owner_ref, pick_ref, traces_ref, gram_ref, sems):
    tiles = out_ref.shape[0]
    slots = foot_ref.shape[1]
    frames = rec_ref.shape[1]
    half = slots // 2
    active = traces_ref.shape[0]
    copies = start(
        sems,
        [
            (foot_hbm, foot_ref),
            (rec_hbm, rec_ref),
            (owner_hbm, owner_ref),
            (pick_hbm, pick_ref),
            (traces_hbm.at[pl.ds(0, active), :], traces_ref),
        ],
    )
    for copy in copies:
        copy.wait()
    foot = foot_ref[...]
    both = dot(foot, jnp.concatenate([foot, rec_ref[...]], axis=1), 0, 0)
    gram, drive = both[:, :slots], both[:, slots:].T.astype(BF)
    bound = jnp.sum(jnp.abs(gram), axis=0, keepdims=True)
    high = bound.astype(BF).astype(F32)
    middle = (bound - high).astype(BF).astype(F32)
    low = bound - high - middle
    named = [high, middle, low, owner_ref[...].astype(F32), pick_ref[...].astype(F32)]
    rest = jnp.zeros((META - len(named), slots), F32)
    tail = jnp.concatenate([traces_ref[...]] + named + [rest], axis=0).astype(BF)
    gram_ref[...] = gram.astype(BF)
    gram = gram_ref[pl.ds(pl.multiple_of(core_ref[0] * half, 16), half), :]
    for tile in range(tiles):
        out_ref[tile, 0:half, :] = gram
        out_ref[tile, half : half + frames, :] = drive
        out_ref[tile, half + frames : half + frames + active + META, :] = tail


def index_of(tail, active):
    meta = tail[active : active + META]
    return meta[3:4] * float(active) + meta[4:5]


def begin_kernel(tile_ref, got_ref, traces_hbm, pick_ref, pull_ref, scale_ref, cur_ref, first_ref, sems):
    tiles, rows, slots = got_ref.shape
    frames = cur_ref.shape[0]
    half = slots // 2
    active = rows - half - frames - META
    count = tiles * active
    row = lax.broadcasted_iota(jnp.int32, (count, slots), 0).astype(F32)
    for tile in range(tiles):
        tail = got_ref[place(tile, tiles), half + frames :, :].astype(F32)
        first_ref[tile * active : (tile + 1) * active, :] = tail[:active]
        pick_ref[tile] = jnp.where(row == index_of(tail, active), 1.0, 0.0).astype(BF)
    at = pl.multiple_of(tile_ref[0] * active, 8)
    copies = start(sems, [(traces_hbm.at[pl.ds(0, active), :], first_ref.at[pl.ds(at, active), :])])
    pick = jnp.concatenate([pick_ref[tile] for tile in range(tiles)], axis=1)
    parts = jnp.concatenate([got_ref[place(tile, tiles), half:, :] for tile in range(tiles)], axis=1)
    sums = dot(parts, pick, 1, 1)
    pull_ref[...] = sums[:frames]
    bound = sums[frames + active : frames + active + META]
    scale_ref[...] = jnp.broadcast_to(1.0 / (1.0 + bound[0:1] + bound[1:2] + bound[2:3]), scale_ref.shape)
    for copy in copies:
        copy.wait()
    cur_ref[...] = first_ref[...].T


def trace_kernel(core_ref, tile_ref, got_ref, far_ref, near_ref, pick_ref, pull_ref, scale_ref, cur_ref, new_ref, own_ref, gram_ref, first_ref, both_ref, drawn_ref):
    tiles, count, slots = pick_ref.shape
    half = slots // 2
    frames = cur_ref.shape[0]
    active = count // tiles
    core = core_ref[0]
    here = pl.multiple_of(core * half, 16)
    there = pl.multiple_of((1 - core) * half, 16)
    mixed, parts = [], []
    for tile in range(tiles):
        spot = place(tile, tiles)
        gram_ref[tile, pl.ds(here, half), :] = got_ref[spot, :half, :]
        gram_ref[tile, pl.ds(there, half), :] = far_ref[spot, :half, :]
        first_ref[tile * active : (tile + 1) * active, :] = far_ref[spot, half + frames :, :].astype(F32)[:active]
        parts.append(far_ref[spot, half : half + frames, :])
        mixed.append(dot(pick_ref[tile], gram_ref[tile], 1, 0).astype(BF))
    first_ref[pl.ds(pl.multiple_of(tile_ref[0] * active, 8), active), :] = near_ref[...]
    pick = jnp.concatenate([pick_ref[tile] for tile in range(tiles)], axis=1)
    whole = dot(jnp.concatenate(mixed, axis=1), pick, 1, 1).astype(BF)
    both_ref[core] = cur_ref[...]
    both_ref[1 - core] = first_ref[...].T
    drawn_ref[core] = pull_ref[...]
    drawn_ref[1 - core] = dot(jnp.concatenate(parts, axis=1), pick, 1, 1)
    pull = jnp.concatenate([drawn_ref[0], drawn_ref[1]], axis=0)
    current = jnp.concatenate([both_ref[0], both_ref[1]], axis=0)
    scale = scale_ref[0:1, :]
    for _ in range(ITER_C):
        push = dot(current.astype(BF), whole, 1, 0)
        current = jnp.maximum(current - (push - pull) * scale, 0.0)
    own_ref[...] = dot(current.astype(BF), pick_ref[tile_ref[0]], 1, 0).astype(BF)
    both_ref[0], both_ref[1] = current[:frames], current[frames:]
    new_ref[...] = both_ref[core]


def trace_steps_wide(got, far, near, owner, pick, traces, me, core):
    tiles, _, slots = got.shape
    half = slots // 2
    active = traces.shape[0] // 8
    frames = traces.shape[1]
    count = tiles * active
    spots = jnp.array([place(tile, tiles) for tile in range(tiles)])
    got, far = jnp.take(got, spots, axis=0), jnp.take(far, spots, axis=0)
    tail = got[:, half + frames :].astype(F32)
    index = jax.vmap(lambda t: index_of(t, active))(tail).astype(jnp.int32).reshape(tiles, slots)
    bound = jnp.sum(tail[:, active : active + 3], axis=1).reshape(-1)
    bound = jax.ops.segment_sum(bound, index.reshape(-1), num_segments=count)
    scale = (1.0 / (1.0 + bound))[:, None]

    def in_order(ours, others, axis):
        return jnp.where(core == 0, jnp.concatenate([ours, others], axis=axis), jnp.concatenate([others, ours], axis=axis))

    def rows_of(block, exact):
        rows = block[:, half + frames : half + frames + active].astype(F32).reshape(count, frames)
        return lax.dynamic_update_slice(rows, exact, (me * active, 0))

    def step(_, current):
        def add(total, parts):
            ours, others, rows = parts
            gram = in_order(ours[:half], others[:half], 0).astype(F32)
            drive = in_order(ours[half : half + frames], others[half : half + frames], 0).astype(F32).T
            terms = dot(gram, jnp.take(current, rows, axis=0), 1, 0, HIGHEST) - drive
            return total.at[rows].add(terms), None

        total, _ = lax.scan(add, jnp.zeros_like(current), (got, far, index))
        return jnp.maximum(current - total * scale, 0.0)

    current = lax.fori_loop(0, ITER_C, step, in_order(rows_of(got, traces[:active]), rows_of(far, near), 1))
    own = jnp.take(current, owner[0] * active + pick[0], axis=0)
    mine = lax.dynamic_slice(current, (me * active, core * frames), (active, frames))
    return mine.T, own.T.astype(BF)


def line_up_kernel(spot_ref, *refs):
    parts, out_ref = refs[:-1], refs[-1]
    for offset, part in enumerate(parts):
        out_ref[spot_ref[0] ^ offset] = part[...]


def pair_sums(lane, rec_ref, own):
    first = lane & -2
    rec = jnp.concatenate([rec_ref[first], rec_ref[first + 1]], axis=1)
    return dot(own, own, 0, 0), dot(rec, own, 1, 0)


def early_kernel(spot_ref, tile_ref, traces_ref, cur_ref, rec_ref, own_ref, new_hbm, gram_ref, data_ref, all_ref, new_ref, sems):
    owned = new_ref.shape[0]
    active = owned // 8
    all_ref[...] = cur_ref[...].T
    at = pl.multiple_of(tile_ref[0] * active if cur_ref.shape[1] > active else 0, 8)
    new_ref[:active, :] = all_ref[pl.ds(at, active), :]
    new_ref[active:, :] = jnp.maximum(traces_ref[active:, :], 0.0)
    copies = start(sems, [(new_ref, new_hbm)])
    gram_ref[...], data_ref[...] = pair_sums(spot_ref[0], rec_ref, own_ref[...])
    for copy in copies:
        copy.wait()


def sweep_kernel(spot_ref, foot_ref, rec_ref, gram_ref, data_ref, *refs):
    lanes = rec_ref.shape[0]
    own_refs, refs = refs[: lanes // 2 - 1], refs[lanes // 2 - 1 :]
    out_hbm, out_ref, now_ref, add_ref, sems = refs
    voxels, slots = foot_ref.shape
    gram, data = gram_ref[...], data_ref[...]
    for offset, own_ref in zip(range(2, lanes, 2), own_refs):
        more, extra = pair_sums(spot_ref[0] ^ offset, rec_ref, own_ref[...])
        gram, data = gram + more, data + extra
    step = 1.0 / (1.0 + jnp.sum(jnp.abs(gram), axis=0, keepdims=True))
    mix = jnp.concatenate(split(gram * step), axis=1)
    foot = foot_ref[...].astype(F32)
    add_ref[...] = jnp.where(foot > 0, data * step, OFF)
    now_ref[...] = foot

    def swept(part):
        now = now_ref[part, :]
        moved = dot(now.astype(BF), mix, 1, 0)
        return jnp.maximum(now - (moved[:, :slots] + moved[:, slots:]) + add_ref[part, :], 0.0)

    for _ in range(ITER_A - 1):
        now_ref[...] = swept(slice(None))
    size = voxels // BLOCKS
    copies = []
    for block in range(BLOCKS):
        out_ref[block * size : (block + 1) * size, :] = swept(slice(block * size, (block + 1) * size)).astype(BF)
        part = pl.ds(block * size, size)
        copies += start(sems.at[pl.ds(block, 1)], [(out_ref.at[part, :], out_hbm.at[part, :])])
    for copy in copies:
        copy.wait()


def body(recording, footprints, slot_owner, slot_pick, traces):
    tiles = lax.axis_size("tile")
    lanes = lax.axis_size("frame")
    voxels, slots = footprints.shape
    owned, frames = traces.shape
    active = owned // 8
    half = slots // 2
    count = tiles * active
    me = lax.axis_index("tile").astype(jnp.int32)[None]
    spot = lax.axis_index("frame").astype(jnp.int32)[None]
    core = spot & 1
    owner = slot_owner.reshape(1, slots)
    pick = slot_pick.reshape(1, slots)
    rows = half + frames + active + META

    def swap(value, bit):
        return lax.ppermute(value, "frame", [(i, i ^ bit) for i in range(lanes)])

    def shape(dims, dtype=F32):
        return jax.ShapeDtypeStruct(dims, dtype)

    packed = pl.pallas_call(
        pack_kernel,
        out_shape=shape((tiles, rows, slots), BF),
        in_specs=[SMEM] + [HBM] * 5,
        out_specs=VMEM,
        scratch_shapes=[
            pltpu.VMEM((voxels, slots), BF),
            pltpu.VMEM((voxels, frames), BF),
            pltpu.VMEM((1, slots), jnp.int32),
            pltpu.VMEM((1, slots), jnp.int32),
            pltpu.VMEM((active, frames), F32),
            pltpu.VMEM((slots, slots), BF),
            pltpu.SemaphoreType.DMA((5,)),
        ],
        name="pack",
    )(core, footprints, recording, owner, pick, traces)
    got = lax.all_to_all(packed, "tile", split_axis=0, concat_axis=0, axis_index_groups=[order_of(tiles)], tiled=True)

    blocks = [recording] + [swap(recording, bit) for bit in range(2, lanes, 2)]
    blocks = [part for block in blocks for part in (block, swap(block, 1))]
    lined = pl.pallas_call(
        line_up_kernel,
        out_shape=shape((lanes, voxels, frames), BF),
        in_specs=[SMEM] + [VMEM] * lanes,
        out_specs=VMEM,
        compiler_params=PARAMS,
        name="line_up",
    )(spot, *blocks)
    near = swap(traces[:active], 1)
    got, lined, near = lax.optimization_barrier((got, lined, near))
    far = swap(got, 1)
    if count <= DENSE_LIMIT:
        begun = pl.pallas_call(
            begin_kernel,
            out_shape=(
                shape((tiles, count, slots), BF),
                shape((frames, count)),
                shape((8, count)),
                shape((frames, count)),
            ),
            in_specs=[SMEM, VMEM, HBM],
            out_specs=(VMEM,) * 4,
            scratch_shapes=[pltpu.VMEM((count, frames), F32), pltpu.SemaphoreType.DMA((1,))],
            compiler_params=PARAMS,
            name="begin",
        )(me, got, traces)
        current, own = pl.pallas_call(
            trace_kernel,
            out_shape=(shape((frames, count)), shape((2 * frames, slots), BF)),
            in_specs=[SMEM] * 2 + [VMEM] * 7,
            out_specs=(VMEM,) * 2,
            scratch_shapes=[
                pltpu.VMEM((tiles, slots, slots), BF),
                pltpu.VMEM((count, frames), F32),
                pltpu.VMEM((2, frames, count), F32),
                pltpu.VMEM((2, frames, count), F32),
            ],
            compiler_params=PARAMS,
            name="traces",
        )(core, me, got, far, near, *begun)
    else:
        current, own = trace_steps_wide(got, far, near, owner, pick, traces, me[0], core[0])
    others = [swap(own, bit) for bit in range(2, lanes, 2)]
    new_traces, gram, data = pl.pallas_call(
        early_kernel,
        out_shape=(shape((owned, frames)), shape((slots, slots)), shape((voxels, slots))),
        in_specs=[SMEM] * 2 + [VMEM] * 4,
        out_specs=(HBM, VMEM, VMEM),
        scratch_shapes=[
            pltpu.VMEM(current.shape[::-1], F32),
            pltpu.VMEM((owned, frames), F32),
            pltpu.SemaphoreType.DMA((1,)),
        ],
        compiler_params=PARAMS,
        name="early",
    )(spot, me, traces, current, lined, own)
    updated = pl.pallas_call(
        sweep_kernel,
        out_shape=shape((voxels, slots), BF),
        in_specs=[SMEM] + [VMEM] * (4 + len(others)),
        out_specs=HBM,
        scratch_shapes=[
            pltpu.VMEM((voxels, slots), BF),
            pltpu.VMEM((voxels, slots), F32),
            pltpu.VMEM((voxels, slots), F32),
            pltpu.SemaphoreType.DMA((BLOCKS,)),
        ],
        compiler_params=PARAMS,
        name="sweeps",
    )(spot, footprints, lined, gram, data, *others)
    return (new_traces, updated)


def solution(mesh):
    in_specs = (P("tile", "frame"), P("tile", None), P("tile", None), P("tile"), P("tile", "frame"))
    out_specs = (P("tile", "frame"), P("tile", None))
    return jax.shard_map(body, mesh=mesh, in_specs=in_specs, out_specs=out_specs, check_vma=False)
```

```python
import jax
import jax.numpy as jnp
from jax import lax
from jax.experimental import pallas as pl
from jax.experimental.pallas import tpu as pltpu
from jax.sharding import PartitionSpec as P

ITER_C = 4
ITER_A = 8
META = 8
BLOCKS = 4
DENSE_LIMIT = 1024
OFF = -1e30
BF = jnp.bfloat16
F32 = jnp.float32
VMEM = pl.BlockSpec(memory_space=pltpu.VMEM)
SMEM = pl.BlockSpec(memory_space=pltpu.SMEM)
HBM = pl.BlockSpec(memory_space=pltpu.MemorySpace.HBM)
HIGHEST = lax.Precision.HIGHEST
PARAMS = pltpu.CompilerParams(vmem_limit_bytes=16 << 20)


def dot(a, b, ca, cb, precision=None):
    return lax.dot_general(a, b, (((ca,), (cb,)), ((), ())), precision=precision, preferred_element_type=F32)


def split(x):
    high = x.astype(BF)
    return high, (x - high.astype(F32)).astype(BF)


def order_of(tiles):
    return sorted(range(tiles), key=lambda tile: (tile % 2, (tiles // 2 - tile + tile % 2) % tiles))


def place(source, tiles):
    return order_of(tiles).index(source)


def start(sems, pairs):
    copies = [pltpu.make_async_copy(source, target, sems.at[i]) for i, (source, target) in enumerate(pairs)]
    for copy in copies:
        copy.start()
    return copies


def pack_kernel(core_ref, foot_hbm, rec_hbm, owner_hbm, pick_hbm, traces_hbm, out_ref, foot_ref, rec_ref, owner_ref, pick_ref, traces_ref, gram_ref, sems):
    tiles = out_ref.shape[0]
    slots = foot_ref.shape[1]
    frames = rec_ref.shape[1]
    half = slots // 2
    active = traces_ref.shape[0]
    copies = start(
        sems,
        [
            (foot_hbm, foot_ref),
            (rec_hbm, rec_ref),
            (owner_hbm, owner_ref),
            (pick_hbm, pick_ref),
            (traces_hbm.at[pl.ds(0, active), :], traces_ref),
        ],
    )
    for copy in copies:
        copy.wait()
    foot = foot_ref[...]
    both = dot(foot, jnp.concatenate([foot, rec_ref[...]], axis=1), 0, 0)
    gram, drive = both[:, :slots], both[:, slots:].T.astype(BF)
    bound = jnp.sum(jnp.abs(gram), axis=0, keepdims=True)
    high = bound.astype(BF).astype(F32)
    middle = (bound - high).astype(BF).astype(F32)
    low = bound - high - middle
    named = [high, middle, low, owner_ref[...].astype(F32), pick_ref[...].astype(F32)]
    rest = jnp.zeros((META - len(named), slots), F32)
    tail = jnp.concatenate([traces_ref[...]] + named + [rest], axis=0).astype(BF)
    lane = lax.broadcasted_iota(jnp.int32, (half, slots), 1)
    gram_ref[:half, :] = jnp.where(lane < half, 0.5 * gram[:half], gram[:half]).astype(BF)
    fold = jnp.where(lane[: half // 2] < half, pltpu.roll(gram[half : half + half // 2], half, 1), gram[half + half // 2 :])
    gram_ref[half:, :] = (0.5 * fold).astype(BF)
    piece = out_ref.shape[1] - frames - active - META
    gram = gram_ref[pl.ds(pl.multiple_of(core_ref[0] * piece, 16), piece), :]
    for tile in range(tiles):
        out_ref[tile, 0:piece, :] = gram
        out_ref[tile, piece : piece + frames, :] = drive
        out_ref[tile, piece + frames : piece + frames + active + META, :] = tail


def index_of(tail, active):
    meta = tail[active : active + META]
    return meta[3:4] * float(active) + meta[4:5]


def begin_kernel(tile_ref, got_ref, traces_hbm, pick_ref, pull_ref, scale_ref, cur_ref, first_ref, sems):
    tiles, rows, slots = got_ref.shape
    count, frames = first_ref.shape
    active = count // tiles
    piece = rows - frames - active - META
    row = lax.broadcasted_iota(jnp.int32, (count, slots), 0).astype(F32)
    for tile in range(tiles):
        tail = got_ref[place(tile, tiles), piece + frames :, :].astype(F32)
        first_ref[tile * active : (tile + 1) * active, :] = tail[:active]
        pick_ref[tile] = jnp.where(row == index_of(tail, active), 1.0, 0.0).astype(BF)
    at = pl.multiple_of(tile_ref[0] * active, 8)
    copies = start(sems, [(traces_hbm.at[pl.ds(0, active), :], first_ref.at[pl.ds(at, active), :])])
    pick = jnp.concatenate([pick_ref[tile] for tile in range(tiles)], axis=1)
    parts = jnp.concatenate([got_ref[place(tile, tiles), piece:, :] for tile in range(tiles)], axis=1)
    sums = dot(parts, pick, 1, 1)
    pull_ref[...] = sums[:frames]
    bound = sums[frames + active : frames + active + META]
    scale_ref[...] = jnp.broadcast_to(1.0 / (1.0 + bound[0:1] + bound[1:2] + bound[2:3]), scale_ref.shape)
    for copy in copies:
        copy.wait()
    cur_ref[...] = first_ref[...].T


def trace_kernel(core_ref, tile_ref, got_ref, far_ref, near_ref, pick_ref, pull_ref, scale_ref, cur_ref, new_ref, own_ref, gram_ref, first_ref, both_ref, drawn_ref):
    tiles, count, slots = pick_ref.shape
    half = slots // 2
    frames = cur_ref.shape[0]
    active = count // tiles
    piece = got_ref.shape[1] - frames - active - META
    core = core_ref[0]
    here = pl.multiple_of(core * piece, 16)
    there = pl.multiple_of((1 - core) * piece, 16)
    right = lax.broadcasted_iota(jnp.int32, (half // 2, slots), 1) >= half
    mixed, parts = [], []
    for tile in range(tiles):
        spot = place(tile, tiles)
        gram_ref[tile, pl.ds(here, piece), :] = got_ref[spot, :piece, :]
        gram_ref[tile, pl.ds(there, piece), :] = far_ref[spot, :piece, :]
        first_ref[tile * active : (tile + 1) * active, :] = far_ref[spot, piece + frames :, :].astype(F32)[:active]
        parts.append(far_ref[spot, piece : piece + frames, :])
        fold = gram_ref[tile, half:, :].astype(F32)
        lower = jnp.concatenate([jnp.where(right, pltpu.roll(fold, half, 1), 0.0), jnp.where(right, fold, 0.0)], axis=0)
        upper = jnp.concatenate([gram_ref[tile, :half, :], lower.astype(BF)], axis=0)
        mixed.append(dot(pick_ref[tile], upper, 1, 0).astype(BF))
    first_ref[pl.ds(pl.multiple_of(tile_ref[0] * active, 8), active), :] = near_ref[...]
    pick = jnp.concatenate([pick_ref[tile] for tile in range(tiles)], axis=1)
    whole = dot(jnp.concatenate(mixed, axis=1), pick, 1, 1)
    whole = (whole + whole.T).astype(BF)
    both_ref[core] = cur_ref[...]
    both_ref[1 - core] = first_ref[...].T
    drawn_ref[core] = pull_ref[...]
    drawn_ref[1 - core] = dot(jnp.concatenate(parts, axis=1), pick, 1, 1)
    pull = jnp.concatenate([drawn_ref[0], drawn_ref[1]], axis=0)
    current = jnp.concatenate([both_ref[0], both_ref[1]], axis=0)
    scale = scale_ref[0:1, :]
    for _ in range(ITER_C):
        push = dot(current.astype(BF), whole, 1, 0)
        current = jnp.maximum(current - (push - pull) * scale, 0.0)
    own_ref[...] = dot(current.astype(BF), pick_ref[tile_ref[0]], 1, 0).astype(BF)
    both_ref[0], both_ref[1] = current[:frames], current[frames:]
    new_ref[...] = both_ref[core]


def trace_steps_wide(got, far, near, owner, pick, traces, me, core):
    tiles, _, slots = got.shape
    half = slots // 2
    piece = 3 * slots // 8
    active = traces.shape[0] // 8
    frames = traces.shape[1]
    count = tiles * active
    spots = jnp.array([place(tile, tiles) for tile in range(tiles)])
    got, far = jnp.take(got, spots, axis=0), jnp.take(far, spots, axis=0)
    tail = got[:, piece + frames :].astype(F32)
    index = jax.vmap(lambda t: index_of(t, active))(tail).astype(jnp.int32).reshape(tiles, slots)
    bound = jnp.sum(tail[:, active : active + 3], axis=1).reshape(-1)
    bound = jax.ops.segment_sum(bound, index.reshape(-1), num_segments=count)
    scale = (1.0 / (1.0 + bound))[:, None]

    def in_order(ours, others, axis):
        return jnp.where(core == 0, jnp.concatenate([ours, others], axis=axis), jnp.concatenate([others, ours], axis=axis))

    def rows_of(block, exact):
        rows = block[:, piece + frames : piece + frames + active].astype(F32).reshape(count, frames)
        return lax.dynamic_update_slice(rows, exact, (me * active, 0))

    def step(_, current):
        def add(total, parts):
            ours, others, rows = parts
            upper = in_order(ours[:piece], others[:piece], 0).astype(F32)
            fold = jnp.concatenate([upper[half:, :half], upper[half:, half:]], axis=0)
            gram = jnp.concatenate([upper[:half], jnp.pad(fold, ((0, 0), (half, 0)))], axis=0)
            gram = gram + gram.T
            drive = in_order(ours[piece : piece + frames], others[piece : piece + frames], 0).astype(F32).T
            terms = dot(gram, jnp.take(current, rows, axis=0), 1, 0, HIGHEST) - drive
            return total.at[rows].add(terms), None

        total, _ = lax.scan(add, jnp.zeros_like(current), (got, far, index))
        return jnp.maximum(current - total * scale, 0.0)

    current = lax.fori_loop(0, ITER_C, step, in_order(rows_of(got, traces[:active]), rows_of(far, near), 1))
    own = jnp.take(current, owner[0] * active + pick[0], axis=0)
    mine = lax.dynamic_slice(current, (me * active, core * frames), (active, frames))
    return mine.T, own.T.astype(BF)


def line_up_kernel(spot_ref, *refs):
    parts, out_ref = refs[:-1], refs[-1]
    for offset, part in enumerate(parts):
        out_ref[spot_ref[0] ^ offset] = part[...]


def pair_sums(lane, rec_ref, own):
    first = lane & -2
    rec = jnp.concatenate([rec_ref[first], rec_ref[first + 1]], axis=1)
    return dot(own, own, 0, 0), dot(rec, own, 1, 0)


def early_kernel(spot_ref, tile_ref, traces_ref, cur_ref, rec_ref, own_ref, new_hbm, gram_ref, data_ref, all_ref, new_ref, sems):
    owned = new_ref.shape[0]
    active = owned // 8
    all_ref[...] = cur_ref[...].T
    at = pl.multiple_of(tile_ref[0] * active if cur_ref.shape[1] > active else 0, 8)
    new_ref[:active, :] = all_ref[pl.ds(at, active), :]
    new_ref[active:, :] = jnp.maximum(traces_ref[active:, :], 0.0)
    copies = start(sems, [(new_ref, new_hbm)])
    gram_ref[...], data_ref[...] = pair_sums(spot_ref[0], rec_ref, own_ref[...])
    for copy in copies:
        copy.wait()


def sweep_kernel(spot_ref, foot_ref, rec_ref, gram_ref, data_ref, *refs):
    lanes = rec_ref.shape[0]
    own_refs, refs = refs[: lanes // 2 - 1], refs[lanes // 2 - 1 :]
    out_hbm, out_ref, now_ref, add_ref, sems = refs
    voxels, slots = foot_ref.shape
    gram, data = gram_ref[...], data_ref[...]
    for offset, own_ref in zip(range(2, lanes, 2), own_refs):
        more, extra = pair_sums(spot_ref[0] ^ offset, rec_ref, own_ref[...])
        gram, data = gram + more, data + extra
    step = 1.0 / (1.0 + jnp.sum(jnp.abs(gram), axis=0, keepdims=True))
    mix = jnp.concatenate(split(gram * step), axis=1)
    foot = foot_ref[...].astype(F32)
    add_ref[...] = jnp.where(foot > 0, data * step, OFF)
    now_ref[...] = foot

    def swept(part):
        now = now_ref[part, :]
        moved = dot(now.astype(BF), mix, 1, 0)
        return jnp.maximum(now - (moved[:, :slots] + moved[:, slots:]) + add_ref[part, :], 0.0)

    for _ in range(ITER_A - 1):
        now_ref[...] = swept(slice(None))
    size = voxels // BLOCKS
    copies = []
    for block in range(BLOCKS):
        out_ref[block * size : (block + 1) * size, :] = swept(slice(block * size, (block + 1) * size)).astype(BF)
        part = pl.ds(block * size, size)
        copies += start(sems.at[pl.ds(block, 1)], [(out_ref.at[part, :], out_hbm.at[part, :])])
    for copy in copies:
        copy.wait()


def body(recording, footprints, slot_owner, slot_pick, traces):
    tiles = lax.axis_size("tile")
    lanes = lax.axis_size("frame")
    voxels, slots = footprints.shape
    owned, frames = traces.shape
    active = owned // 8
    piece = 3 * slots // 8
    count = tiles * active
    me = lax.axis_index("tile").astype(jnp.int32)[None]
    spot = lax.axis_index("frame").astype(jnp.int32)[None]
    core = spot & 1
    owner = slot_owner.reshape(1, slots)
    pick = slot_pick.reshape(1, slots)
    rows = piece + frames + active + META

    def swap(value, bit):
        return lax.ppermute(value, "frame", [(i, i ^ bit) for i in range(lanes)])

    def shape(dims, dtype=F32):
        return jax.ShapeDtypeStruct(dims, dtype)

    packed = pl.pallas_call(
        pack_kernel,
        out_shape=shape((tiles, rows, slots), BF),
        in_specs=[SMEM] + [HBM] * 5,
        out_specs=VMEM,
        scratch_shapes=[
            pltpu.VMEM((voxels, slots), BF),
            pltpu.VMEM((voxels, frames), BF),
            pltpu.VMEM((1, slots), jnp.int32),
            pltpu.VMEM((1, slots), jnp.int32),
            pltpu.VMEM((active, frames), F32),
            pltpu.VMEM((2 * piece, slots), BF),
            pltpu.SemaphoreType.DMA((5,)),
        ],
        name="pack",
    )(core, footprints, recording, owner, pick, traces)
    got = lax.all_to_all(packed, "tile", split_axis=0, concat_axis=0, axis_index_groups=[order_of(tiles)], tiled=True)

    blocks = [recording] + [swap(recording, bit) for bit in range(2, lanes, 2)]
    blocks = [part for block in blocks for part in (block, swap(block, 1))]
    lined = pl.pallas_call(
        line_up_kernel,
        out_shape=shape((lanes, voxels, frames), BF),
        in_specs=[SMEM] + [VMEM] * lanes,
        out_specs=VMEM,
        compiler_params=PARAMS,
        name="line_up",
    )(spot, *blocks)
    near = swap(traces[:active], 1)
    got, lined, near = lax.optimization_barrier((got, lined, near))
    far = swap(got, 1)
    if count <= DENSE_LIMIT:
        begun = pl.pallas_call(
            begin_kernel,
            out_shape=(
                shape((tiles, count, slots), BF),
                shape((frames, count)),
                shape((8, count)),
                shape((frames, count)),
            ),
            in_specs=[SMEM, VMEM, HBM],
            out_specs=(VMEM,) * 4,
            scratch_shapes=[pltpu.VMEM((count, frames), F32), pltpu.SemaphoreType.DMA((1,))],
            compiler_params=PARAMS,
            name="begin",
        )(me, got, traces)
        current, own = pl.pallas_call(
            trace_kernel,
            out_shape=(shape((frames, count)), shape((2 * frames, slots), BF)),
            in_specs=[SMEM] * 2 + [VMEM] * 7,
            out_specs=(VMEM,) * 2,
            scratch_shapes=[
                pltpu.VMEM((tiles, 2 * piece, slots), BF),
                pltpu.VMEM((count, frames), F32),
                pltpu.VMEM((2, frames, count), F32),
                pltpu.VMEM((2, frames, count), F32),
            ],
            compiler_params=PARAMS,
            name="traces",
        )(core, me, got, far, near, *begun)
    else:
        current, own = trace_steps_wide(got, far, near, owner, pick, traces, me[0], core[0])
    others = [swap(own, bit) for bit in range(2, lanes, 2)]
    new_traces, gram, data = pl.pallas_call(
        early_kernel,
        out_shape=(shape((owned, frames)), shape((slots, slots)), shape((voxels, slots))),
        in_specs=[SMEM] * 2 + [VMEM] * 4,
        out_specs=(HBM, VMEM, VMEM),
        scratch_shapes=[
            pltpu.VMEM(current.shape[::-1], F32),
            pltpu.VMEM((owned, frames), F32),
            pltpu.SemaphoreType.DMA((1,)),
        ],
        compiler_params=PARAMS,
        name="early",
    )(spot, me, traces, current, lined, own)
    updated = pl.pallas_call(
        sweep_kernel,
        out_shape=shape((voxels, slots), BF),
        in_specs=[SMEM] + [VMEM] * (4 + len(others)),
        out_specs=HBM,
        scratch_shapes=[
            pltpu.VMEM((voxels, slots), BF),
            pltpu.VMEM((voxels, slots), F32),
            pltpu.VMEM((voxels, slots), F32),
            pltpu.SemaphoreType.DMA((BLOCKS,)),
        ],
        compiler_params=PARAMS,
        name="sweeps",
    )(spot, footprints, lined, gram, data, *others)
    return (new_traces, updated)


def solution(mesh):
    in_specs = (P("tile", "frame"), P("tile", None), P("tile", None), P("tile"), P("tile", "frame"))
    out_specs = (P("tile", "frame"), P("tile", None))
    return jax.shard_map(body, mesh=mesh, in_specs=in_specs, out_specs=out_specs, check_vma=False)
```

```python
import jax
import jax.numpy as jnp
from jax import lax
from jax.experimental import pallas as pl
from jax.experimental.pallas import tpu as pltpu
from jax.sharding import PartitionSpec as P


ITER_C = 4
ITER_A = 8
META = 8
BLOCKS = 4
DENSE_LIMIT = 1024
OFF = -1e30
BF = jnp.bfloat16
F32 = jnp.float32
VMEM = pl.BlockSpec(memory_space=pltpu.VMEM)
SMEM = pl.BlockSpec(memory_space=pltpu.SMEM)
HBM = pl.BlockSpec(memory_space=pltpu.MemorySpace.HBM)
HIGHEST = lax.Precision.HIGHEST
PARAMS = pltpu.CompilerParams(vmem_limit_bytes=16 << 20)


def dot(a, b, ca, cb, precision=None):
    return lax.dot_general(a, b, (((ca,), (cb,)), ((), ())), precision=precision, preferred_element_type=F32)


def split(x):
    high = x.astype(BF)
    return high, (x - high.astype(F32)).astype(BF)


def order_of(tiles):
    return sorted(range(tiles), key=lambda tile: (tile % 2, (tiles // 2 - tile + tile % 2) % tiles))


def place(source, tiles):
    return order_of(tiles).index(source)


def start(sems, pairs):
    copies = [pltpu.make_async_copy(source, target, sems.at[i]) for i, (source, target) in enumerate(pairs)]
    for copy in copies:
        copy.start()
    return copies


def pack_kernel(core_ref, foot_hbm, rec_hbm, owner_hbm, pick_hbm, traces_hbm, out_ref, foot_ref, rec_ref, owner_ref, pick_ref, traces_ref, gram_ref, sems):
    tiles = out_ref.shape[0]
    slots = foot_ref.shape[1]
    frames = rec_ref.shape[1]
    half = slots // 2
    active = traces_ref.shape[0]
    copies = start(
        sems,
        [
            (foot_hbm, foot_ref),
            (rec_hbm, rec_ref),
            (owner_hbm, owner_ref),
            (pick_hbm, pick_ref),
            (traces_hbm.at[pl.ds(0, active), :], traces_ref),
        ],
    )
    for copy in copies:
        copy.wait()
    foot = foot_ref[...]
    both = dot(foot, jnp.concatenate([foot, rec_ref[...]], axis=1), 0, 0)
    gram, drive = both[:, :slots], both[:, slots:].T.astype(BF)
    bound = jnp.sum(jnp.abs(gram), axis=0, keepdims=True)
    high = bound.astype(BF).astype(F32)
    middle = (bound - high).astype(BF).astype(F32)
    low = bound - high - middle
    named = [high, middle, low, owner_ref[...].astype(F32), pick_ref[...].astype(F32)]
    rest = jnp.zeros((META - len(named), slots), F32)
    tail = jnp.concatenate([traces_ref[...]] + named + [rest], axis=0).astype(BF)
    lane = lax.broadcasted_iota(jnp.int32, (half, slots), 1)
    gram_ref[:half, :] = jnp.where(lane < half, 0.5 * gram[:half], gram[:half]).astype(BF)
    fold = jnp.where(lane[: half // 2] < half, pltpu.roll(gram[half : half + half // 2], half, 1), gram[half + half // 2 :])
    gram_ref[half:, :] = (0.5 * fold).astype(BF)
    piece = out_ref.shape[1] - frames - active - META
    gram = gram_ref[pl.ds(pl.multiple_of(core_ref[0] * piece, 16), piece), :]
    for tile in range(tiles):
        out_ref[tile, 0:piece, :] = gram
        out_ref[tile, piece : piece + frames, :] = drive
        out_ref[tile, piece + frames : piece + frames + active + META, :] = tail


def index_of(tail, active):
    meta = tail[active : active + META]
    return meta[3:4] * float(active) + meta[4:5]


def begin_kernel(tile_ref, got_ref, traces_hbm, pick_ref, pull_ref, scale_ref, cur_ref, first_ref, sems):
    tiles, rows, slots = got_ref.shape
    count, frames = first_ref.shape
    active = count // tiles
    piece = rows - frames - active - META
    row = lax.broadcasted_iota(jnp.int32, (count, slots), 0).astype(F32)
    for tile in range(tiles):
        tail = got_ref[place(tile, tiles), piece + frames :, :].astype(F32)
        first_ref[tile * active : (tile + 1) * active, :] = tail[:active]
        pick_ref[tile] = jnp.where(row == index_of(tail, active), 1.0, 0.0).astype(BF)
    at = pl.multiple_of(tile_ref[0] * active, 8)
    copies = start(sems, [(traces_hbm.at[pl.ds(0, active), :], first_ref.at[pl.ds(at, active), :])])
    pick = jnp.concatenate([pick_ref[tile] for tile in range(tiles)], axis=1)
    parts = jnp.concatenate([got_ref[place(tile, tiles), piece:, :] for tile in range(tiles)], axis=1)
    sums = dot(parts, pick, 1, 1)
    pull_ref[...] = sums[:frames]
    bound = sums[frames + active : frames + active + META]
    scale_ref[...] = jnp.broadcast_to(1.0 / (1.0 + bound[0:1] + bound[1:2] + bound[2:3]), scale_ref.shape)
    for copy in copies:
        copy.wait()
    cur_ref[...] = first_ref[...].T


def trace_kernel(core_ref, tile_ref, got_ref, far_ref, near_ref, pick_ref, pull_ref, scale_ref, cur_ref, new_ref, own_ref, gram_ref, first_ref, both_ref, drawn_ref):
    tiles, count, slots = pick_ref.shape
    half = slots // 2
    frames = cur_ref.shape[0]
    active = count // tiles
    piece = got_ref.shape[1] - frames - active - META
    core = core_ref[0]
    here = pl.multiple_of(core * piece, 16)
    there = pl.multiple_of((1 - core) * piece, 16)
    right = lax.broadcasted_iota(jnp.int32, (half // 2, slots), 1) >= half
    mixed, parts = [], []
    for tile in range(tiles):
        spot = place(tile, tiles)
        gram_ref[tile, pl.ds(here, piece), :] = got_ref[spot, :piece, :]
        gram_ref[tile, pl.ds(there, piece), :] = far_ref[spot, :piece, :]
        first_ref[tile * active : (tile + 1) * active, :] = far_ref[spot, piece + frames :, :].astype(F32)[:active]
        parts.append(far_ref[spot, piece : piece + frames, :])
        fold = gram_ref[tile, half:, :].astype(F32)
        lower = jnp.concatenate([jnp.where(right, pltpu.roll(fold, half, 1), 0.0), jnp.where(right, fold, 0.0)], axis=0)
        upper = jnp.concatenate([gram_ref[tile, :half, :], lower.astype(BF)], axis=0)
        mixed.append(dot(pick_ref[tile], upper, 1, 0).astype(BF))
    first_ref[pl.ds(pl.multiple_of(tile_ref[0] * active, 8), active), :] = near_ref[...]
    pick = jnp.concatenate([pick_ref[tile] for tile in range(tiles)], axis=1)
    whole = dot(jnp.concatenate(mixed, axis=1), pick, 1, 1)
    whole = (whole + whole.T).astype(BF)
    both_ref[core] = cur_ref[...]
    both_ref[1 - core] = first_ref[...].T
    drawn_ref[core] = pull_ref[...]
    drawn_ref[1 - core] = dot(jnp.concatenate(parts, axis=1), pick, 1, 1)
    pull = jnp.concatenate([drawn_ref[0], drawn_ref[1]], axis=0)
    current = jnp.concatenate([both_ref[0], both_ref[1]], axis=0)
    scale = scale_ref[0:1, :]
    for _ in range(ITER_C):
        push = dot(current.astype(BF), whole, 1, 0)
        current = jnp.maximum(current - (push - pull) * scale, 0.0)
    own_ref[...] = dot(current.astype(BF), pick_ref[tile_ref[0]], 1, 0).astype(BF)
    both_ref[0], both_ref[1] = current[:frames], current[frames:]
    new_ref[...] = both_ref[core]


def trace_steps_wide(got, far, near, owner, pick, traces, me, core):
    tiles, _, slots = got.shape
    half = slots // 2
    piece = 3 * slots // 8
    active = traces.shape[0] // 8
    frames = traces.shape[1]
    count = tiles * active
    spots = jnp.array([place(tile, tiles) for tile in range(tiles)])
    got, far = jnp.take(got, spots, axis=0), jnp.take(far, spots, axis=0)
    tail = got[:, piece + frames :].astype(F32)
    index = jax.vmap(lambda t: index_of(t, active))(tail).astype(jnp.int32).reshape(tiles, slots)
    bound = jnp.sum(tail[:, active : active + 3], axis=1).reshape(-1)
    bound = jax.ops.segment_sum(bound, index.reshape(-1), num_segments=count)
    scale = (1.0 / (1.0 + bound))[:, None]

    def in_order(ours, others, axis):
        return jnp.where(core == 0, jnp.concatenate([ours, others], axis=axis), jnp.concatenate([others, ours], axis=axis))

    def rows_of(block, exact):
        rows = block[:, piece + frames : piece + frames + active].astype(F32).reshape(count, frames)
        return lax.dynamic_update_slice(rows, exact, (me * active, 0))

    def step(_, current):
        def add(total, parts):
            ours, others, rows = parts
            upper = in_order(ours[:piece], others[:piece], 0).astype(F32)
            fold = jnp.concatenate([upper[half:, :half], upper[half:, half:]], axis=0)
            gram = jnp.concatenate([upper[:half], jnp.pad(fold, ((0, 0), (half, 0)))], axis=0)
            gram = gram + gram.T
            drive = in_order(ours[piece : piece + frames], others[piece : piece + frames], 0).astype(F32).T
            terms = dot(gram, jnp.take(current, rows, axis=0), 1, 0, HIGHEST) - drive
            return total.at[rows].add(terms), None

        total, _ = lax.scan(add, jnp.zeros_like(current), (got, far, index))
        return jnp.maximum(current - total * scale, 0.0)

    current = lax.fori_loop(0, ITER_C, step, in_order(rows_of(got, traces[:active]), rows_of(far, near), 1))
    own = jnp.take(current, owner[0] * active + pick[0], axis=0)
    mine = lax.dynamic_slice(current, (me * active, core * frames), (active, frames))
    return mine.T, own.T.astype(BF)


def pair_sums(lane, ours_ref, others_ref, rec_ref, own):
    rec_ref[lane & 1] = ours_ref[...]
    rec_ref[1 - (lane & 1)] = others_ref[...]
    return dot(own, own, 0, 0), dot(jnp.concatenate([rec_ref[0], rec_ref[1]], axis=1), own, 1, 0)


def early_kernel(spot_ref, tile_ref, traces_ref, cur_ref, own_ref, ours_ref, others_ref, new_hbm, gram_ref, data_ref, all_ref, rec_ref, new_ref, sems):
    owned = new_ref.shape[0]
    active = owned // 8
    all_ref[...] = cur_ref[...].T
    at = pl.multiple_of(tile_ref[0] * active if cur_ref.shape[1] > active else 0, 8)
    new_ref[:active, :] = all_ref[pl.ds(at, active), :]
    new_ref[active:, :] = jnp.maximum(traces_ref[active:, :], 0.0)
    copies = start(sems, [(new_ref, new_hbm)])
    gram_ref[...], data_ref[...] = pair_sums(spot_ref[0], ours_ref, others_ref, rec_ref, own_ref[...])
    for copy in copies:
        copy.wait()


def sweep_kernel(spot_ref, foot_ref, gram_ref, data_ref, *refs):
    far_refs, refs = refs[:-6], refs[-6:]
    out_hbm, rec_ref, out_ref, now_ref, add_ref, sems = refs
    voxels, slots = foot_ref.shape
    gram, data = gram_ref[...], data_ref[...]
    for at in range(0, len(far_refs), 3):
        own_ref, ours_ref, others_ref = far_refs[at : at + 3]
        more, extra = pair_sums(spot_ref[0], ours_ref, others_ref, rec_ref, own_ref[...])
        gram, data = gram + more, data + extra
    step = 1.0 / (1.0 + jnp.sum(jnp.abs(gram), axis=0, keepdims=True))
    mix = jnp.concatenate(split(gram * step), axis=1)
    foot = foot_ref[...].astype(F32)
    add_ref[...] = jnp.where(foot > 0, data * step, OFF)
    now_ref[...] = foot

    def swept(part):
        now = now_ref[part, :]
        moved = dot(now.astype(BF), mix, 1, 0)
        return jnp.maximum(now - (moved[:, :slots] + moved[:, slots:]) + add_ref[part, :], 0.0)

    for _ in range(ITER_A - 1):
        now_ref[...] = swept(slice(None))
    size = voxels // BLOCKS
    copies = []
    for block in range(BLOCKS):
        out_ref[block * size : (block + 1) * size, :] = swept(slice(block * size, (block + 1) * size)).astype(BF)
        part = pl.ds(block * size, size)
        copies += start(sems.at[pl.ds(block, 1)], [(out_ref.at[part, :], out_hbm.at[part, :])])
    for copy in copies:
        copy.wait()


def body(recording, footprints, slot_owner, slot_pick, traces):
    tiles = lax.axis_size("tile")
    lanes = lax.axis_size("frame")
    voxels, slots = footprints.shape
    owned, frames = traces.shape
    active = owned // 8
    piece = 3 * slots // 8
    count = tiles * active
    me = lax.axis_index("tile").astype(jnp.int32)[None]
    spot = lax.axis_index("frame").astype(jnp.int32)[None]
    core = spot & 1
    owner = slot_owner.reshape(1, slots)
    pick = slot_pick.reshape(1, slots)
    rows = piece + frames + active + META

    def swap(value, bit):
        return lax.ppermute(value, "frame", [(i, i ^ bit) for i in range(lanes)])

    def shape(dims, dtype=F32):
        return jax.ShapeDtypeStruct(dims, dtype)

    packed = pl.pallas_call(
        pack_kernel,
        out_shape=shape((tiles, rows, slots), BF),
        in_specs=[SMEM] + [HBM] * 5,
        out_specs=VMEM,
        scratch_shapes=[
            pltpu.VMEM((voxels, slots), BF),
            pltpu.VMEM((voxels, frames), BF),
            pltpu.VMEM((1, slots), jnp.int32),
            pltpu.VMEM((1, slots), jnp.int32),
            pltpu.VMEM((active, frames), F32),
            pltpu.VMEM((2 * piece, slots), BF),
            pltpu.SemaphoreType.DMA((5,)),
        ],
        name="pack",
    )(core, footprints, recording, owner, pick, traces)
    got = lax.all_to_all(packed, "tile", split_axis=0, concat_axis=0, axis_index_groups=[order_of(tiles)], tiled=True)

    hops = range(2, lanes, 2)
    beside = swap(recording, 1)
    across = [swap(recording, hop) for hop in hops]
    passed = [swap(block, 1) for block in across]
    near = swap(traces[:active], 1)
    got, near, beside, across = lax.optimization_barrier((got, near, beside, across))
    far = swap(got, 1)
    if count <= DENSE_LIMIT:
        begun = pl.pallas_call(
            begin_kernel,
            out_shape=(
                shape((tiles, count, slots), BF),
                shape((frames, count)),
                shape((8, count)),
                shape((frames, count)),
            ),
            in_specs=[SMEM, VMEM, HBM],
            out_specs=(VMEM,) * 4,
            scratch_shapes=[pltpu.VMEM((count, frames), F32), pltpu.SemaphoreType.DMA((1,))],
            compiler_params=PARAMS,
            name="begin",
        )(me, got, traces)
        current, own = pl.pallas_call(
            trace_kernel,
            out_shape=(shape((frames, count)), shape((2 * frames, slots), BF)),
            in_specs=[SMEM] * 2 + [VMEM] * 7,
            out_specs=(VMEM,) * 2,
            scratch_shapes=[
                pltpu.VMEM((tiles, 2 * piece, slots), BF),
                pltpu.VMEM((count, frames), F32),
                pltpu.VMEM((2, frames, count), F32),
                pltpu.VMEM((2, frames, count), F32),
            ],
            compiler_params=PARAMS,
            name="traces",
        )(core, me, got, far, near, *begun)
    else:
        current, own = trace_steps_wide(got, far, near, owner, pick, traces, me[0], core[0])
    far_own = [swap(own, hop) for hop in hops]
    far_sides = [part for parts in zip(far_own, across, passed) for part in parts]
    new_traces, gram, data = pl.pallas_call(
        early_kernel,
        out_shape=(shape((owned, frames)), shape((slots, slots)), shape((voxels, slots))),
        in_specs=[SMEM] * 2 + [VMEM] * 5,
        out_specs=(HBM, VMEM, VMEM),
        scratch_shapes=[
            pltpu.VMEM(current.shape[::-1], F32),
            pltpu.VMEM((2, voxels, frames), BF),
            pltpu.VMEM((owned, frames), F32),
            pltpu.SemaphoreType.DMA((1,)),
        ],
        compiler_params=PARAMS,
        name="early",
    )(spot, me, traces, current, own, recording, beside)
    updated = pl.pallas_call(
        sweep_kernel,
        out_shape=shape((voxels, slots), BF),
        in_specs=[SMEM] + [VMEM] * (3 + len(far_sides)),
        out_specs=HBM,
        scratch_shapes=[
            pltpu.VMEM((2, voxels, frames), BF),
            pltpu.VMEM((voxels, slots), BF),
            pltpu.VMEM((voxels, slots), F32),
            pltpu.VMEM((voxels, slots), F32),
            pltpu.SemaphoreType.DMA((BLOCKS,)),
        ],
        compiler_params=PARAMS,
        name="sweeps",
    )(spot, footprints, gram, data, *far_sides)
    return (new_traces, updated)


def solution(mesh):
    in_specs = (P("tile", "frame"), P("tile", None), P("tile", None), P("tile"), P("tile", "frame"))
    out_specs = (P("tile", "frame"), P("tile", None))
    return jax.shard_map(body, mesh=mesh, in_specs=in_specs, out_specs=out_specs, check_vma=False)
```
